32 devices in a mesh: gx: 4 (over y, core), gy: 4 (over z), gz: 2 (over x).
Axes of the slice: x: 2, y: 2, z: 4, core: 2. Of those that a mesh axis runs over, the one named last changes fastest.
Arguments:
- thermal_anomaly: float32 [64, 64, 256], P('gx', 'gy', 'gz'), may hold values from -6 to 6
- specific_vapour: float32 [64, 64, 256], P('gx', 'gy', 'gz'), may hold values from -6 to 6
- server_thermal_load: float32 [64, 64, 256], P('gx', 'gy', 'gz'), may hold values from -5 to 5
- lateral_mixing_coefficient: float32 [64, 64, 256], P('gx', 'gy', 'gz'), may hold values from 40 to 800
- upward_mixing_coefficient: float32 [64, 64, 256], P('gx', 'gy', 'gz'), may hold values from 0.1 to 0.25
- cfl_along_lateral_axis: float32 [64, 64, 256], P('gx', 'gy', 'gz'), may hold values from -30 to 30
- cfl_across_lateral_axis: float32 [64, 64, 256], P('gx', 'gy', 'gz'), may hold values from -30 to 30
- cfl_upward_axis: float32 [64, 64, 256], P('gx', 'gy', 'gz'), may hold values from -0.15 to 0.15
Outputs:
- temperature_new: float32 [64, 64, 256], P('gx', 'gy', 'gz')
- humidity_new: float32 [64, 64, 256], P('gx', 'gy', 'gz')
The draws below stay inside these ranges and needn't reach their ends.
All inputs are finite; a program needn't handle non-finite values.
Results may differ from the reference program's by a relative error of at most 0.0003.
Values sent between devices are 32-bit elements; how exact they have to be, the bound alone decides.
No kernel may reach another device: no remote copies, remote signals or barrier semaphores. Data moves between devices by JAX's collectives and lax.ppermute only.
A program may use at most 64 MiB of HBM per device.

```python
import math
import jax
import jax.numpy as jnp
from jax import lax

NX = 64
NY = 64
NZ = 256


def smooth_part(key):
    keys = jax.random.split(key, 3)
    phases = jax.random.uniform(keys[0], (4,), jnp.float32, 0.0, 6.2831853)
    amps = jax.random.uniform(keys[1], (4,), jnp.float32, 0.4, 0.8)
    first = (jnp.arange(NX, dtype=jnp.float32) * (6.2831853 / NX)).reshape(NX, 1, 1)
    second = (jnp.arange(NY, dtype=jnp.float32) * (6.2831853 / NY)).reshape(1, NY, 1)
    plane = amps[0] * jnp.sin(first + phases[0]) * jnp.cos(second + phases[1]) + amps[1] * jnp.sin(2.0 * first + phases[2]) + amps[2] * jnp.cos(2.0 * second + phases[3]) + amps[3] * jnp.sin(first + second + phases[1] - phases[2])
    column = jax.random.uniform(keys[2], (1, 1, NZ), jnp.float32, 0.5, 1.5)
    return plane * column


def field_normal(key):
    keys = jax.random.split(key, 2)
    rough = jax.random.normal(keys[0], (NX, NY, NZ), jnp.float32)
    return jnp.clip(0.8 * rough + smooth_part(keys[1]), -6.0, 6.0)


def draw_thermal_anomaly(key, part):
    inner = jax.random.fold_in(key, 11)
    return field_normal(inner)


def draw_specific_vapour(key, part):
    inner = jax.random.fold_in(key, 23)
    return field_normal(inner)


def draw_server_thermal_load(key, part):
    inner = jax.random.fold_in(key, 37)
    keys = jax.random.split(inner, 3)
    factor = jax.random.uniform(keys[0], (NX, NY, NZ), jnp.float32, 0.5, 1.5)
    rough = 0.25 * jax.random.normal(keys[1], (NX, NY, NZ), jnp.float32)
    smooth = smooth_part(keys[2])
    return jnp.clip(smooth * factor + rough, -5.0, 5.0)


def block_levels(own_key, dims, cuts, smallest, high):
    level = 1.0
    for dim, blocks in cuts:
        draws = jax.random.uniform(jax.random.fold_in(jax.random.fold_in(own_key, 6), dim), (blocks,), jnp.float32, smallest / len(cuts), high / len(cuts))
        level = level * jnp.repeat(jnp.exp(draws), dims[dim] // blocks).reshape((-1,) + (1,) * (len(dims) - 1 - dim))
    return level


def setup_inputs(seed: int = 0) -> dict:
    arg_keys = jax.random.split(jax.random.key(seed), 9)
    thermal_anomaly = draw_thermal_anomaly(jax.random.fold_in(arg_keys[8], 71), 0)
    specific_vapour = draw_specific_vapour(jax.random.fold_in(arg_keys[8], 71), 0)
    server_thermal_load = draw_server_thermal_load(jax.random.fold_in(arg_keys[8], 71), 0)
    lateral_mixing_coefficient = jnp.clip(jnp.exp(math.log(800.0) - 2.9957323 * jax.random.uniform(arg_keys[3], (NX, NY, NZ), jnp.float32) ** block_levels(arg_keys[3], (NX, NY, NZ), ((0, 4), (1, 4), (2, 2)), -0.2, 0.2)), 40.0, 800.0)
    upward_mixing_coefficient = jnp.clip(jnp.exp(math.log(0.25) - 0.9162907 * jax.random.uniform(arg_keys[4], (NX, NY, NZ), jnp.float32) ** block_levels(arg_keys[4], (NX, NY, NZ), ((0, 4), (1, 4), (2, 2)), -0.2, 0.2)), 0.1, 0.25)
    cfl_along_lateral_axis = jnp.clip(jax.random.uniform(arg_keys[5], (NX, NY, NZ), jnp.float32, -30.0, 30.0) * block_levels(arg_keys[5], (NX, NY, NZ), ((0, 4), (1, 4), (2, 2)), -0.4, 0.0), -30.0, 30.0)
    cfl_across_lateral_axis = jnp.clip(jax.random.uniform(arg_keys[6], (NX, NY, NZ), jnp.float32, -30.0, 30.0) * block_levels(arg_keys[6], (NX, NY, NZ), ((0, 4), (1, 4), (2, 2)), -0.4, 0.0), -30.0, 30.0)
    cfl_upward_axis = jnp.clip(jax.random.uniform(arg_keys[7], (NX, NY, NZ), jnp.float32, -0.15, 0.15) * block_levels(arg_keys[7], (NX, NY, NZ), ((0, 4), (1, 4), (2, 2)), -0.4, 0.0), -0.15, 0.15)
    return dict(thermal_anomaly=thermal_anomaly, specific_vapour=specific_vapour, server_thermal_load=server_thermal_load, lateral_mixing_coefficient=lateral_mixing_coefficient, upward_mixing_coefficient=upward_mixing_coefficient, cfl_along_lateral_axis=cfl_along_lateral_axis, cfl_across_lateral_axis=cfl_across_lateral_axis, cfl_upward_axis=cfl_upward_axis)


vapour_scaling = 0.8


def shifted_ahead(prior_tracer, position):
    length = prior_tracer.shape[position]
    inner = lax.slice_in_dim(prior_tracer, 1, length, axis=position)
    zeros = jnp.zeros_like(lax.slice_in_dim(prior_tracer, 0, 1, axis=position))
    return jnp.concatenate([inner, zeros], axis=position)


def shifted_behind(prior_tracer, position):
    length = prior_tracer.shape[position]
    inner = lax.slice_in_dim(prior_tracer, 0, length - 1, axis=position)
    zeros = jnp.zeros_like(lax.slice_in_dim(prior_tracer, 0, 1, axis=position))
    return jnp.concatenate([zeros, inner], axis=position)


def explicit(prior_tracer, east_coef, west_coef, position):
    ahead = shifted_ahead(prior_tracer, position) - prior_tracer
    behind = shifted_behind(prior_tracer, position) - prior_tracer
    return east_coef * ahead + west_coef * behind


def solve_lines(east_coef, west_coef, right_side):
    lower_band = -west_coef
    diagonal_band = 1.0 + east_coef + west_coef
    upper_band = -east_coef

    def forward(carried, cell_data):
        upper_before, right_before = carried
        lower_cell, diagonal_cell, upper_cell, right_cell = cell_data
        pivots = diagonal_cell - lower_cell * upper_before
        upper_now = upper_cell / pivots
        right_now = (right_cell - lower_cell * right_before) / pivots
        return (upper_now, right_now), (upper_now, right_now)

    start = (jnp.zeros_like(right_side[0]), jnp.zeros_like(right_side[0]))
    unused, ratios = lax.scan(forward, start, (lower_band, diagonal_band, upper_band, right_side))

    def backward(value_after, cell_data):
        upper_ratio, right_ratio = cell_data
        value = right_ratio - upper_ratio * value_after
        return value, value

    unused_end, values = lax.scan(backward, jnp.zeros_like(right_side[0]), ratios, reverse=True)
    return values


def reference(thermal_anomaly, specific_vapour, server_thermal_load, lateral_mixing_coefficient, upward_mixing_coefficient, cfl_along_lateral_axis, cfl_across_lateral_axis, cfl_upward_axis):
    results = []
    for scaling_element, prior_tracer, coefficient_element in ((1.0, thermal_anomaly, 1.0), (vapour_scaling, specific_vapour, 0.0)):
        east_x = scaling_element * lateral_mixing_coefficient - 0.5 * cfl_along_lateral_axis
        west_x = scaling_element * lateral_mixing_coefficient + 0.5 * cfl_along_lateral_axis
        east_y = scaling_element * lateral_mixing_coefficient - 0.5 * cfl_across_lateral_axis
        west_y = scaling_element * lateral_mixing_coefficient + 0.5 * cfl_across_lateral_axis
        east_z = scaling_element * upward_mixing_coefficient - 0.5 * cfl_upward_axis
        west_z = scaling_element * upward_mixing_coefficient + 0.5 * cfl_upward_axis
        source = coefficient_element * server_thermal_load
        first_side = prior_tracer + explicit(prior_tracer, east_y, west_y, 1) + explicit(prior_tracer, east_z, west_z, 2) + source
        half_field = solve_lines(east_x, west_x, first_side)
        second_side = half_field + explicit(half_field, east_x, west_x, 0) + explicit(half_field, east_z, west_z, 2) + source
        moved = solve_lines(jnp.moveaxis(east_y, 1, 0), jnp.moveaxis(west_y, 1, 0), jnp.moveaxis(second_side, 1, 0))
        results.append(jnp.moveaxis(moved, 0, 1))
    return (results[0], results[1])
```

```python
import functools

import jax
import jax.numpy as jnp
from jax import lax
from jax.experimental import pallas as pl
from jax.experimental.pallas import tpu as pltpu
from jax.sharding import PartitionSpec as P

RATIOS = (1.0, 0.8)
F32 = jnp.float32
EXACT = lax.Precision.HIGHEST


def vmem():
    return pl.BlockSpec(memory_space=pltpu.VMEM)


def call(kernel, outs, *args, scratch=(), flops=400000):
    size = sum(4 * a.size for a in args)
    return pl.pallas_call(
        kernel,
        out_shape=tuple(jax.ShapeDtypeStruct(s, F32) for s in outs),
        in_specs=[vmem()] * len(args),
        out_specs=tuple(vmem() for _ in outs),
        scratch_shapes=list(scratch),
        cost_estimate=pl.CostEstimate(flops=flops, bytes_accessed=size, transcendentals=0),
    )(*args)


def factor(n, lat, half_cfl, ratio, inv_out, mid_out, up_out, first_out, last_out):
    inv, mids, ups, firsts = [], [], [], []
    up = first = None
    for k in range(n):
        lateral = ratio * lat(k)
        half = half_cfl(k)
        east, west = lateral - half, lateral + half
        pivot = 1.0 + 2.0 * lateral
        if k:
            pivot = pivot - west * up
        inverse = 1.0 / pivot
        mid = west * inverse
        up = east * inverse
        first = mid if k == 0 else mid * first
        inv_out(k, inverse)
        mid_out(k, mid)
        up_out(k, up)
        ups.append(up)
        firsts.append(first)
    q, r = firsts[-1], ups[-1]
    first_out(n - 1, q)
    last_out(n - 1, r)
    for k in range(n - 2, -1, -1):
        q = firsts[k] + ups[k] * q
        r = ups[k] * r
        first_out(k, q)
        last_out(k, r)


def sweep(n, rhs, inv, mid, up, out):
    values = []
    value = None
    for k in range(n):
        value = inv(k) * rhs(k) if k == 0 else inv(k) * rhs(k) + mid(k) * value
        values.append(value)
    out(n - 1, value)
    for k in range(n - 2, -1, -1):
        value = values[k] + up(k) * value
        out(k, value)


def along(port, before):
    p1, p2, q1, q2, r1, r2 = port
    source, slope = before
    t = 1.0 / (1.0 - q1 * slope)
    step = q2 * slope * t
    return (p2 + q2 * source + step * (p1 + q1 * source), r2 + step * r1)


def mirrored(port):
    p1, p2, q1, q2, r1, r2 = port
    return (p2, p1, r2, r1, q2, q1)


def interface(me, n, port_of, own):
    zero = jnp.zeros_like(own[0])
    left, right = (zero, zero), (zero, zero)
    for j in range(n - 1):
        stepped = along(port_of(j), left)
        left = tuple(jnp.where(j < me, a, b) for a, b in zip(stepped, left))
        i = n - 1 - j
        stepped = along(mirrored(port_of(i)), right)
        right = tuple(jnp.where(i > me, a, b) for a, b in zip(stepped, right))
    p1, p2, q1, q2, r1, r2 = own
    pl_, ql = left
    pr, qr = right
    a1 = p1 + q1 * pl_ + r1 * pr
    a2 = p2 + q2 * pl_ + r2 * pr
    b11, b22 = 1.0 - q1 * ql, 1.0 - r2 * qr
    b12, b21 = r1 * qr, q2 * ql
    t = 1.0 / (b11 * b22 - b12 * b21)
    u1 = (a1 * b22 + b12 * a2) * t
    u2 = (b11 * a2 + b21 * a1) * t
    return pl_ + ql * u1, pr + qr * u2


def faces_kernel(nx, ny, nz, t_ref, h_ref, odd_y, fy1, fy2, fz):
    pass


def strided(ref, f, k, nx, ny):
    return ref[f, pl.ds(k, nx, stride=ny), :]


def coef_kernel(nx, ny, lat, cx, cy, xi, xm, xu, xq, xr, yi, ym, yu, yq, yr):
    def put(ref, f):
        def store(k, v):
            ref[f, k] = v

        return store

    for f, ratio in enumerate(RATIOS):
        factor(
            nx,
            lambda k: lat[pl.ds(k * ny, ny), :],
            lambda k: 0.5 * cx[pl.ds(k * ny, ny), :],
            ratio,
            *(put(ref, f) for ref in (xi, xm, xu, xq, xr)),
        )
        factor(
            ny,
            lambda k: lat[pl.ds(k, nx, stride=ny), :],
            lambda k: 0.5 * cy[pl.ds(k, nx, stride=ny), :],
            ratio,
            *(put(ref, f) for ref in (yi, ym, yu, yq, yr)),
        )


def lane_shifts(v, nz, high, low):
    lane = lax.broadcasted_iota(jnp.int32, v.shape, v.ndim - 1)
    ahead = jnp.where(lane == nz - 1, high, pltpu.roll(v, nz - 1, v.ndim - 1))
    behind = jnp.where(lane == 0, low, pltpu.roll(v, 1, v.ndim - 1))
    return ahead, behind


def first_kernel(nx, ny, nz, t, h, load, lat, up, cy, cz, ylo, yhi, zlo, zhi, xi, xm, xu, d, p):
    for f, (ratio, ref) in enumerate(zip(RATIOS, (t, h))):
        for k in range(nx):
            v = ref[k]
            row = lax.broadcasted_iota(jnp.int32, v.shape, 0)
            ahead = jnp.where(row == ny - 1, yhi[f, pl.ds(k, 1), :], pltpu.roll(v, ny - 1, 0))
            behind = jnp.where(row == 0, ylo[f, pl.ds(k, 1), :], pltpu.roll(v, 1, 0))
            lateral, half = ratio * lat[k], 0.5 * cy[k]
            out = v + ((lateral - half) * (ahead - v) + (lateral + half) * (behind - v))
            ahead, behind = lane_shifts(v, nz, zhi[f, k], zlo[f, k])
            lateral, half = ratio * up[k], 0.5 * cz[k]
            out = out + ((lateral - half) * (ahead - v) + (lateral + half) * (behind - v))
            if f == 0:
                out = out + load[k]
            d[f, k] = out

        def put(k, v):
            p[f, k] = v

        sweep(nx, lambda k: d[f, k], lambda k: xi[f, k], lambda k: xm[f, k], lambda k: xu[f, k], put)


def own_port(ref, f):
    return tuple(ref[v, f] for v in range(6))


def half_kernel(axis, n, by_xor, nx, p, q, r, ports, own, half):
    me = lax.axis_index(axis)
    for f in range(2):

        def port_of(j):
            at = (j ^ me) if by_xor else j
            return tuple(ports[at, v, f] for v in range(6))

        low, high = interface(me, n, port_of, own_port(own, f))
        for k in range(nx):
            half[f, k] = p[f, k] + q[f, k] * low + r[f, k] * high


def second_kernel(nx, ny, nz, half, d, load, up, cz, zlo, zhi, yi, ym, yu, p, s):
    for f, ratio in enumerate(RATIOS):
        for k in range(nx):
            v = half[f, k]
            ahead, behind = lane_shifts(v, nz, zhi[f, k], zlo[f, k])
            lateral, half_cfl = ratio * up[k], 0.5 * cz[k]
            out = 2.0 * v - d[f, k]
            out = out + ((lateral - half_cfl) * (ahead - v) + (lateral + half_cfl) * (behind - v))
            if f == 0:
                out = out + load[k]
            s[f, pl.ds(k * ny, ny), :] = out

        def put(k, v):
            p[f, k] = v

        sweep(
            ny,
            lambda k: s[f, pl.ds(k, nx, stride=ny), :],
            lambda k: yi[f, k],
            lambda k: ym[f, k],
            lambda k: yu[f, k],
            put,
        )


def new_kernel(axis, n, by_xor, nx, ny, p, q, r, ports, own, t_new, h_new):
    me = lax.axis_index(axis)
    for f, ref in enumerate((t_new, h_new)):

        def port_of(j):
            at = (j ^ me) if by_xor else j
            return tuple(ports[at, v, f] for v in range(6))

        low, high = interface(me, n, port_of, own_port(own, f))
        for k in range(ny):
            ref[pl.ds(k, nx, stride=ny), :] = p[f, k] + q[f, k] * low + r[f, k] * high


def neighbours(low_face, high_face, axis):
    n = lax.axis_size(axis)
    even = lax.axis_index(axis) % 2 == 0

    def swap(pairs, value):
        if not pairs:
            return jnp.zeros_like(value)
        return lax.ppermute(value, axis, pairs + [(b, a) for a, b in pairs])

    one = swap([(i, i + 1) for i in range(0, n - 1, 2)], jnp.where(even, high_face, low_face))
    two = swap([(i, i + 1) for i in range(1, n - 1, 2)], jnp.where(even, low_face, high_face))
    return jnp.where(even, two, one), jnp.where(even, one, two)


def everyones(own, axis):
    n = lax.axis_size(axis)
    by_xor = n in (2, 4)
    if not by_xor:
        return by_xor, lax.all_gather(own, axis)
    parts = [own]
    for k in range(1, n):
        parts.append(lax.ppermute(own, axis, [(i, i ^ k) for i in range(n)]))
    return by_xor, jnp.stack(parts)


def body(thermal, vapour, load, lat, up, cx, cy, cz):
    nx, ny, nz = thermal.shape
    flat = (nx * ny, nz)
    lines_x, lines_y = (2, nx, ny, nz), (2, ny, nx, nz)
    fields = jnp.stack([thermal, vapour])
    ylo, yhi = neighbours(fields[:, :, 0, :], fields[:, :, ny - 1, :], "gy")
    zlo, zhi = neighbours(fields[:, :, :, 0], fields[:, :, :, nz - 1], "gz")
    xi, xm, xu, xq, xr, yi, ym, yu, yq, yr = call(
        functools.partial(coef_kernel, nx, ny),
        (lines_x,) * 5 + (lines_y,) * 5,
        lat.reshape(flat),
        cx.reshape(flat),
        cy.reshape(flat),
    )
    d, p = call(
        functools.partial(first_kernel, nx, ny, nz),
        (lines_x, lines_x),
        thermal, vapour, load, lat, up, cy, cz, ylo, yhi, zlo[..., None], zhi[..., None], xi, xm, xu,
    )
    own = jnp.stack([p[:, 0], p[:, -1], xq[:, 0], xq[:, -1], xr[:, 0], xr[:, -1]])
    by_xor, ports = everyones(own, "gx")
    (half,) = call(
        functools.partial(half_kernel, "gx", lax.axis_size("gx"), by_xor, nx),
        (lines_x,),
        p, xq, xr, ports, own,
    )
    zlo, zhi = neighbours(half[:, :, :, 0], half[:, :, :, nz - 1], "gz")
    (p,) = call(
        functools.partial(second_kernel, nx, ny, nz),
        (lines_y,),
        half, d, load, up, cz, zlo[..., None], zhi[..., None], yi, ym, yu,
        scratch=[pltpu.VMEM((2,) + flat, F32)],
    )
    own = jnp.stack([p[:, 0], p[:, -1], yq[:, 0], yq[:, -1], yr[:, 0], yr[:, -1]])
    by_xor, ports = everyones(own, "gy")
    t_new, h_new = call(
        functools.partial(new_kernel, "gy", lax.axis_size("gy"), by_xor, nx, ny),
        (flat, flat),
        p, yq, yr, ports, own,
    )
    return t_new.reshape(thermal.shape), h_new.reshape(thermal.shape)


def solution(mesh):
    spec = P("gx", "gy", "gz")
    return jax.shard_map(
        body, mesh=mesh, in_specs=(spec,) * 8, out_specs=(spec, spec), check_vma=False
    )
```

```python
import functools

import jax
import jax.numpy as jnp
from jax import lax
from jax.experimental import pallas as pl
from jax.experimental.pallas import tpu as pltpu
from jax.sharding import PartitionSpec as P

RATIOS = (1.0, 0.8)
F32 = jnp.float32


def vmem():
    return pl.BlockSpec(memory_space=pltpu.VMEM)


def call(kernel, outs, *args, scratch=(), flops=400000, space=pltpu.VMEM):
    size = sum(4 * a.size for a in args)
    return pl.pallas_call(
        kernel,
        out_shape=tuple(jax.ShapeDtypeStruct(s, F32) for s in outs),
        in_specs=[pl.BlockSpec(memory_space=space)] * len(args),
        out_specs=tuple(vmem() for _ in outs),
        scratch_shapes=list(scratch),
        compiler_params=pltpu.CompilerParams(vmem_limit_bytes=8 << 20),
        cost_estimate=pl.CostEstimate(flops=flops, bytes_accessed=size, transcendentals=0),
    )(*args)


def factor(n, lat, half_cfl, ratio, inv_out, mid_out, up_out, first_out, last_out):
    ups, firsts = [], []
    up = first = None
    for k in range(n):
        lateral = ratio * lat(k)
        half = half_cfl(k)
        east, west = lateral - half, lateral + half
        pivot = 1.0 + 2.0 * lateral
        if k:
            pivot = pivot - west * up
        inverse = 1.0 / pivot
        mid = west * inverse
        up = east * inverse
        first = mid if k == 0 else mid * first
        inv_out(k, inverse)
        mid_out(k, mid)
        up_out(k, up)
        ups.append(up)
        firsts.append(first)
    q, r = firsts[-1], ups[-1]
    first_out(n - 1, q)
    last_out(n - 1, r)
    q2, r2 = q, r
    for k in range(n - 2, -1, -1):
        q = firsts[k] + ups[k] * q
        r = ups[k] * r
        first_out(k, q)
        last_out(k, r)
    return q, q2, r, r2


def sweep(n, rhs, inv, mid, up, out):
    values = []
    value = None
    for k in range(n):
        value = inv(k) * rhs(k) if k == 0 else inv(k) * rhs(k) + mid(k) * value
        values.append(value)
    out(n - 1, value)
    last = value
    for k in range(n - 2, -1, -1):
        value = values[k] + up(k) * value
        out(k, value)
    return value, last


def along(port, before):
    p1, p2, q1, q2, r1, r2 = port
    source, slope = before
    t = 1.0 / (1.0 - q1 * slope)
    step = q2 * slope * t
    return p2 + q2 * source + step * (p1 + q1 * source), r2 + step * r1


def mirrored(port):
    p1, p2, q1, q2, r1, r2 = port
    return p2, p1, r2, r1, q2, q1


def pick(flag, a, b):
    return tuple(jnp.where(flag, x, y) for x, y in zip(a, b))


def beside(port, left, right):
    p1, p2, q1, q2, r1, r2 = port
    pl_, ql = left
    pr, qr = right
    a1 = p1 + q1 * pl_ + r1 * pr
    a2 = p2 + q2 * pl_ + r2 * pr
    b11, b22 = 1.0 - q1 * ql, 1.0 - r2 * qr
    b12, b21 = r1 * qr, q2 * ql
    t = 1.0 / (b11 * b22 - b12 * b21)
    u1 = (a1 * b22 + b12 * a2) * t
    u2 = (b11 * a2 + b21 * a1) * t
    return pl_ + ql * u1, pr + qr * u2


def place(axis):
    me = lax.axis_index(axis)
    second = me // 2
    return second == 1, second == me % 2, me % 2


def oriented(axis, ends, coefs, f):
    port = tuple(ends) + tuple(coefs[v, f] for v in range(4))
    return pick(place(axis)[0], mirrored(port), port)


def pair_source(axis, f, ends, own, near):
    outer = place(axis)[1]
    zero = jnp.zeros_like(ends[0])
    mine = oriented(axis, ends, own, f)
    other = oriented(axis, (zero, zero), near, f)
    q1, q2, r1, r2 = pick(outer, other[2:], mine[2:])
    slope = jnp.where(outer, mine[5], other[5])
    step = q2 / (1.0 - q1 * slope)
    part = jnp.where(outer, step * mine[1], mine[1] + step * slope * mine[0])
    return part, r2 + step * slope * r1


def pair_whole(axis, f, ends, near_ends, own, near):
    outer = place(axis)[1]
    mine = oriented(axis, ends, own, f)
    other = oriented(axis, near_ends, near, f)
    first, then = pick(outer, mine, other), pick(outer, other, mine)
    return along(then, (first[1], first[5]))


def pair_values(axis, f, ends, near_ends, own, near, far):
    second, outer, _ = place(axis)
    zero = jnp.zeros_like(ends[0])
    mine = oriented(axis, ends, own, f)
    other = oriented(axis, near_ends, near, f)
    ahead = pick(outer, along(mirrored(other), far), far)
    behind = pick(outer, (zero, zero), (other[1], other[5]))
    back, front = beside(mine, behind, ahead)
    return pick(second, (front, back), (back, front))


def scan_values(axis, f, blocks, ends, own, ports):
    me, n = lax.axis_index(axis), lax.axis_size(axis)
    mine = tuple(ends) + tuple(own[v, f] for v in range(4))
    zero = jnp.zeros_like(mine[0])

    def port_of(j):
        return tuple(ports[j, 2 * f + v] for v in range(2)) + tuple(
            ports[j, 2 * blocks + blocks * v + f] for v in range(4)
        )

    def step(j, sides):
        left, right = sides
        left = pick(j < me, along(port_of(j), left), left)
        i = n - 1 - j
        right = pick(i > me, along(mirrored(port_of(i)), right), right)
        return left, right

    left, right = lax.fori_loop(0, n, step, ((zero, zero), (zero, zero)))
    return beside(mine, left, right)


def everyones(axis, ends, own):
    blocks = own.shape[1]
    return lax.all_gather(
        jnp.concatenate([ends, own.reshape((4 * blocks,) + own.shape[2:])]), axis
    )


def swap(value, axis, k):
    return lax.ppermute(value, axis, [(i, i ^ k) for i in range(lax.axis_size(axis))])


PLANES = ("load", "lat", "up", "cx", "cy", "cz")


def open_kernel(nx, nz, *refs):
    ins, outs, tiles, sems = refs[:8], refs[8:16], refs[16], refs[17]
    copies = [pltpu.make_async_copy(a, b, sems.at[i]) for i, (a, b) in enumerate(zip(ins, outs))]
    for copy in copies:
        copy.start()
    upper = lax.axis_index("gz")
    edge, inner = 1 - upper, 2 - 3 * upper
    planes = [(0, edge), (1, edge), (0, inner), (1, inner)] + [(i, edge) for i in range(2, 8)]
    per_tile = nz // nx
    arrived = set()
    lane = lax.broadcasted_iota(jnp.int32, outs[0].shape[1:], 1)
    for first in range(0, len(planes), per_tile):
        tile = jnp.zeros(outs[0].shape[1:], F32)
        for a, (i, offset) in enumerate(planes[first : first + per_tile]):
            if i not in arrived:
                copies[i].wait()
                arrived.add(i)
            for k in range(nx):
                to = nx * a + k
                shift = lax.rem(offset + (to + nz), nz)
                tile = jnp.where(lane == to, pltpu.roll(outs[i][k], shift, 1), tile)
        tiles[first // per_tile] = tile


def put(ref, f):
    def store(k, v):
        ref[f, k] = v

    return store


def coef_kernel(nx, ny, t, h, lat, cx, cy, xi, xm, xu, xq, xr, yi, ym, yu, yq, yr, xown, yown, one, two):
    even = lax.axis_index("gy") % 2 == 0
    for f, (ratio, ref) in enumerate(zip(RATIOS, (t, h))):
        low = ref[pl.ds(0, nx, stride=ny), :]
        high = ref[pl.ds(ny - 1, nx, stride=ny), :]
        one[f] = jnp.where(even, high, low)
        two[f] = jnp.where(even, low, high)
    for f, ratio in enumerate(RATIOS):
        own = factor(
            nx,
            lambda k: lat[pl.ds(k * ny, ny), :],
            lambda k: 0.5 * cx[pl.ds(k * ny, ny), :],
            ratio,
            *(put(ref, f) for ref in (xi, xm, xu, xq, xr)),
        )
        for v in range(4):
            xown[v, f] = own[v]
        own = factor(
            ny,
            lambda k: lat[pl.ds(k, nx, stride=ny), :],
            lambda k: 0.5 * cy[pl.ds(k, nx, stride=ny), :],
            ratio,
            *(put(ref, f) for ref in (yi, ym, yu, yq, yr)),
        )
        for v in range(4):
            yown[v, f] = own[v]
            one[2 + 2 * v + f] = own[v]


class Ghost:
    def __init__(self, shape, nx):
        self.shape, self.nx = shape, nx
        self.first = lax.broadcasted_iota(jnp.int32, shape, 1) < shape[1] // 2
        self.ratio = jnp.where(self.first, RATIOS[0], RATIOS[1])

    def lane(self, tiles, plane, k):
        at = self.nx * plane + k
        column = tiles[at // self.shape[1], :, at % self.shape[1] : at % self.shape[1] + 1]
        return jnp.broadcast_to(column, self.shape)

    def fields(self, tiles, plane, k):
        return jnp.where(self.first, self.lane(tiles, plane, k), self.lane(tiles, plane + 1, k))

    def named(self, tiles, name, k):
        return self.lane(tiles, 4 + PLANES.index(name), k)

    def row(self, row, k):
        shape = (1, self.shape[1])
        first = lax.broadcasted_iota(jnp.int32, shape, 1) < shape[1] // 2
        a = jnp.broadcast_to(row[:, k : k + 1], shape)
        b = jnp.broadcast_to(row[:, self.nx + k : self.nx + k + 1], shape)
        return jnp.where(first, a, b)


def ghost_kernel(nx, tiles, xown, gi, gm, gu, gq, gr, own):
    ghost = Ghost(tiles.shape[1:], nx)

    def keep(ref):
        def store(k, v):
            ref[k] = v

        return store

    ports = factor(
        nx,
        lambda k: ghost.named(tiles, "lat", k),
        lambda k: 0.5 * ghost.named(tiles, "cx", k),
        ghost.ratio,
        *(keep(ref) for ref in (gi, gm, gu, gq, gr)),
    )
    for v in range(4):
        own[v, 0] = xown[v, 0]
        own[v, 1] = xown[v, 1]
        own[v, 2] = ports[v]


def lateral_step(v, ahead_row, behind_row, lateral, half):
    ny = v.shape[0]
    row = lax.broadcasted_iota(jnp.int32, v.shape, 0)
    ahead = jnp.where(row == ny - 1, ahead_row, pltpu.roll(v, ny - 1, 0))
    behind = jnp.where(row == 0, behind_row, pltpu.roll(v, 1, 0))
    return (lateral - half) * (ahead - v) + (lateral + half) * (behind - v)


def vertical_step(nz, v, column, lateral, half):
    upper = lax.axis_index("gz")
    lane = lax.broadcasted_iota(jnp.int32, v.shape, 1)
    column = jnp.broadcast_to(column, v.shape)
    ahead = jnp.where(lane == nz - 1, jnp.where(upper == 0, column, 0.0), pltpu.roll(v, nz - 1, 1))
    behind = jnp.where(lane == 0, jnp.where(upper == 0, 0.0, column), pltpu.roll(v, 1, 1))
    return (lateral - half) * (ahead - v) + (lateral + half) * (behind - v)


def first_kernel(
    nx, ny, nz, t, h, load, lat, up, cy, cz, one, two, mine, tiles, xi, xm, xu, gi, gm, gu, d, p, gp, ends
):
    even = lax.axis_index("gy") % 2 == 0
    upper = lax.axis_index("gz")
    last = one.shape[0] - 1
    for f, (ratio, ref) in enumerate(zip(RATIOS, (t, h))):
        low_rows = jnp.where(even, two[f], one[f])
        high_rows = jnp.where(even, one[f], two[f])
        for k in range(nx):
            v = ref[k]
            out = v + lateral_step(
                v, high_rows[k : k + 1], low_rows[k : k + 1], ratio * lat[k], 0.5 * cy[k]
            )
            at = nx * f + k
            out = out + vertical_step(nz, v, tiles[0, :, at : at + 1], ratio * up[k], 0.5 * cz[k])
            if f == 0:
                out = out + load[k]
            d[f, k] = out
        ends[2 * f], ends[2 * f + 1] = sweep(
            nx, lambda k: d[f, k], lambda k: xi[f, k], lambda k: xm[f, k], lambda k: xu[f, k], put(p, f)
        )
    ghost = Ghost(tiles.shape[1:], nx)
    low_row = jnp.where(even, two[2], one[last])[ny - 1 : ny]
    high_row = jnp.where(even, one[last], two[2])[0:1]
    sides = []
    for k in range(nx):
        v = ghost.fields(tiles, 0, k)
        out = v + lateral_step(
            v,
            ghost.row(high_row, k),
            ghost.row(low_row, k),
            ghost.ratio * ghost.named(tiles, "lat", k),
            0.5 * ghost.named(tiles, "cy", k),
        )
        inner, here = ghost.fields(tiles, 2, k), ghost.fields(mine, 0, k)
        ahead, behind = jnp.where(upper == 0, inner, here), jnp.where(upper == 0, here, inner)
        lateral, half = ghost.ratio * ghost.named(tiles, "up", k), 0.5 * ghost.named(tiles, "cz", k)
        out = out + ((lateral - half) * (ahead - v) + (lateral + half) * (behind - v))
        sides.append(out + jnp.where(ghost.first, ghost.named(tiles, "load", k), 0.0))

    def keep(k, v):
        gp[k] = v

    ends[4], ends[5] = sweep(
        nx, lambda k: sides[k], lambda k: gi[k], lambda k: gm[k], lambda k: gu[k], keep
    )


def pair_kernel(axis, blocks, ends, near_ends, own, near, out):
    for f in range(blocks):
        source, slope = pair_whole(
            axis, f, (ends[2 * f], ends[2 * f + 1]), (near_ends[2 * f], near_ends[2 * f + 1]), own, near
        )
        if f == 2:
            lane = lax.broadcasted_iota(jnp.int32, source.shape, 1)
            out[4] = jnp.where((lane & 32) == 0, source, slope)
        else:
            out[2 * f] = source
            out[2 * f + 1] = slope


def far_word(far, f):
    if f < 2:
        return far[2 * f], far[2 * f + 1]
    both = far[4]
    lane = lax.broadcasted_iota(jnp.int32, both.shape, 1)
    source = jnp.where((lane & 32) == 0, both, pltpu.roll(both, 32, 1))
    slope = jnp.where((lane & 32) == 0, pltpu.roll(both, both.shape[1] - 32, 1), both)
    return source, slope


def second_kernel(
    paired, nx, ny, nz, p, q, r, gp, gq, gr, ends, near_ends, own, near, far,
    d, load, up, cz, yi, ym, yu, yown, ynear, py, *rest,
):
    outs, s = rest[:-1], rest[-1]

    def values(f):
        mine = (ends[2 * f], ends[2 * f + 1])
        if not paired[0]:
            return scan_values("gx", f, 3, mine, own, far)
        other = (near_ends[2 * f], near_ends[2 * f + 1])
        return pair_values("gx", f, mine, other, own, near, far_word(far, f))

    ghost_low, ghost_high = values(2)
    yends, slopes = [], []
    for f, ratio in enumerate(RATIOS):
        low, high = values(f)
        for k in range(nx):
            v = p[f, k] + q[f, k] * low + r[f, k] * high
            beyond = gp[k] + gq[k] * ghost_low + gr[k] * ghost_high
            at = f * nz // 2
            out = 2.0 * v - d[f, k]
            out = out + vertical_step(nz, v, beyond[:, at : at + 1], ratio * up[k], 0.5 * cz[k])
            if f == 0:
                out = out + load[k]
            s[f, pl.ds(k * ny, ny), :] = out
        mine = sweep(
            ny,
            lambda k: s[f, pl.ds(k, nx, stride=ny), :],
            lambda k: yi[f, k],
            lambda k: ym[f, k],
            lambda k: yu[f, k],
            put(py, f),
        )
        outs[0][2 * f], outs[0][2 * f + 1] = mine
        if paired[1]:
            outs[1][f], slope = pair_source("gy", f, mine, yown, ynear)
            slopes.append(slope)
    if paired[1]:
        outs[1][2] = jnp.where(place("gy")[2] == 0, slopes[0], slopes[1])


def new_kernel(paired, nx, ny, p, q, r, ends, near_ends, own, near, *rest):
    received, news = rest[:-2], rest[-2:]
    for f, ref in enumerate(news):
        mine = (ends[2 * f], ends[2 * f + 1])
        if paired:
            other = (near_ends[2 * f], near_ends[2 * f + 1])
            two, three = received
            slope = jnp.where(place("gy")[2] == f, two[2], three[2])
            low, high = pair_values("gy", f, mine, other, own, near, (two[f] + three[f], slope))
        else:
            low, high = scan_values("gy", f, 2, mine, own, received[0])
        for k in range(ny):
            ref[pl.ds(k, nx, stride=ny), :] = p[f, k] + q[f, k] * low + r[f, k] * high


def neighbours(one, two, axis):
    n = lax.axis_size(axis)

    def swapped(first, value):
        pairs = [(i, i + 1) for i in range(first, n - 1, 2)]
        if not pairs:
            return jnp.zeros_like(value)
        return lax.ppermute(value, axis, pairs + [(b, a) for a, b in pairs])

    return swapped(0, one), swapped(1, two)


def body(thermal, vapour, load, lat, up, cx, cy, cz):
    nx, ny, nz = thermal.shape
    assert lax.axis_size("gz") == 2 and nx * 8 == nz
    flat = (nx * ny, nz)
    lines_x, lines_y = (2, nx, ny, nz), (2, ny, nx, nz)
    block_x, block_y = (ny, nz), (nx, nz)
    paired = (lax.axis_size("gx") == 4, lax.axis_size("gy") == 4)
    thermal, vapour, load, lat, up, cx, cy, cz, mine = call(
        functools.partial(open_kernel, nx, nz),
        (thermal.shape,) * 8 + ((2,) + block_x,),
        *(
            pltpu.with_memory_space_constraint(a, pltpu.HBM)
            for a in (thermal, vapour, load, lat, up, cx, cy, cz)
        ),
        scratch=[pltpu.SemaphoreType.DMA((8,))],
        space=pltpu.HBM,
    )
    tiles = swap(mine, "gz", 1)
    xi, xm, xu, xq, xr, yi, ym, yu, yq, yr, xown, yown, one, two = call(
        functools.partial(coef_kernel, nx, ny),
        (lines_x,) * 5
        + (lines_y,) * 5
        + ((4, 2) + block_x, (4, 2) + block_y, (10,) + block_y, (2,) + block_y),
        *(a.reshape(flat) for a in (thermal, vapour, lat, cx, cy)),
    )
    one = one if paired[1] else one[:2]
    one, two = neighbours(
        jnp.concatenate([one, tiles[:1]]), jnp.concatenate([two, tiles[:1]]), "gy"
    )
    ynear = one[2:10].reshape(yown.shape) if paired[1] else yown
    gi, gm, gu, gq, gr, own = call(
        functools.partial(ghost_kernel, nx),
        ((nx,) + block_x,) * 5 + ((4, 3) + block_x,),
        tiles, xown,
    )
    near = swap(own, "gx", 1) if paired[0] else own
    d, p, gp, ends = call(
        functools.partial(first_kernel, nx, ny, nz),
        (lines_x, lines_x, (nx,) + block_x, (6,) + block_x),
        thermal, vapour, load, lat, up, cy, cz, one, two, mine, tiles, xi, xm, xu, gi, gm, gu,
    )
    if paired[0]:
        near_ends = swap(ends, "gx", 1)
        (word,) = call(
            functools.partial(pair_kernel, "gx", 3), ((5,) + block_x,), ends, near_ends, own, near
        )
        far = swap(word, "gx", 2)
    else:
        near_ends, far = ends, everyones("gx", ends, own)
    py, yends, *outs = call(
        functools.partial(second_kernel, paired, nx, ny, nz),
        (lines_y, (4,) + block_y) + (((3,) + block_y,) if paired[1] else ()),
        p, xq, xr, gp, gq, gr, ends, near_ends, own, near, far,
        d, load, up, cz, yi, ym, yu, yown, ynear,
        scratch=[pltpu.VMEM((2,) + flat, F32)],
    )
    if paired[1]:
        near_ends = swap(yends, "gy", 1)
        received = [swap(outs[0], "gy", 2), swap(outs[0], "gy", 3)]
    else:
        near_ends, received = yends, [everyones("gy", yends, yown)]
    t_new, h_new = call(
        functools.partial(new_kernel, paired[1], nx, ny),
        (flat, flat),
        py, yq, yr, yends, near_ends, yown, ynear, *received,
    )
    return t_new.reshape(thermal.shape), h_new.reshape(thermal.shape)


def solution(mesh):
    spec = P("gx", "gy", "gz")
    return jax.shard_map(
        body, mesh=mesh, in_specs=(spec,) * 8, out_specs=(spec, spec), check_vma=False
    )
```

```python
import functools

import jax
import jax.numpy as jnp
from jax import lax
from jax.experimental import pallas as pl
from jax.experimental.pallas import tpu as pltpu
from jax.sharding import PartitionSpec as P


RATIOS = (1.0, 0.8)
F32 = jnp.float32


def vmem():
    return pl.BlockSpec(memory_space=pltpu.VMEM)


def call(kernel, outs, *args, scratch=(), flops=400000, space=pltpu.VMEM):
    size = sum(4 * a.size for a in args)
    return run(kernel, outs, args, scratch, flops, size, space)


def run(kernel, outs, args, scratch, flops, size, space):
    return pl.pallas_call(
        kernel,
        out_shape=tuple(jax.ShapeDtypeStruct(s, F32) for s in outs),
        in_specs=[pl.BlockSpec(memory_space=space)] * len(args),
        out_specs=tuple(vmem() for _ in outs),
        scratch_shapes=list(scratch),
        compiler_params=pltpu.CompilerParams(vmem_limit_bytes=8 << 20),
        cost_estimate=pl.CostEstimate(flops=flops, bytes_accessed=size, transcendentals=0),
    )(*args)


def factor(n, lat, half_cfl, ratio, inv_out, mid_out, up_out, first_out, last_out):
    ups, firsts = [], []
    up = first = None
    for k in range(n):
        lateral = ratio * lat(k)
        half = half_cfl(k)
        east, west = lateral - half, lateral + half
        pivot = 1.0 + 2.0 * lateral
        if k:
            pivot = pivot - west * up
        inverse = 1.0 / pivot
        mid = west * inverse
        up = east * inverse
        first = mid if k == 0 else mid * first
        inv_out(k, inverse)
        mid_out(k, mid)
        up_out(k, up)
        ups.append(up)
        firsts.append(first)
    q, r = firsts[-1], ups[-1]
    first_out(n - 1, q)
    last_out(n - 1, r)
    q2, r2 = q, r
    for k in range(n - 2, -1, -1):
        q = firsts[k] + ups[k] * q
        r = ups[k] * r
        first_out(k, q)
        last_out(k, r)
    return q, q2, r, r2


def sweep(n, rhs, inv, mid, up, out):
    values = []
    value = None
    for k in range(n):
        value = inv(k) * rhs(k) if k == 0 else inv(k) * rhs(k) + mid(k) * value
        values.append(value)
    out(n - 1, value)
    last = value
    for k in range(n - 2, -1, -1):
        value = values[k] + up(k) * value
        out(k, value)
    return value, last


def along(port, before):
    p1, p2, q1, q2, r1, r2 = port
    source, slope = before
    t = 1.0 / (1.0 - q1 * slope)
    step = q2 * slope * t
    return p2 + q2 * source + step * (p1 + q1 * source), r2 + step * r1


def mirrored(port):
    p1, p2, q1, q2, r1, r2 = port
    return p2, p1, r2, r1, q2, q1


def pick(flag, a, b):
    return tuple(jnp.where(flag, x, y) for x, y in zip(a, b))


def beside(port, left, right):
    p1, p2, q1, q2, r1, r2 = port
    pl_, ql = left
    pr, qr = right
    a1 = p1 + q1 * pl_ + r1 * pr
    a2 = p2 + q2 * pl_ + r2 * pr
    b11, b22 = 1.0 - q1 * ql, 1.0 - r2 * qr
    b12, b21 = r1 * qr, q2 * ql
    t = 1.0 / (b11 * b22 - b12 * b21)
    u1 = (a1 * b22 + b12 * a2) * t
    u2 = (b11 * a2 + b21 * a1) * t
    return pl_ + ql * u1, pr + qr * u2


def place(axis):
    me = lax.axis_index(axis)
    second = me // 2
    return second == 1, second == me % 2, me % 2


def oriented(axis, ends, coefs, f):
    port = tuple(ends) + tuple(coefs[v, f] for v in range(4))
    return pick(place(axis)[0], mirrored(port), port)


def pair_source(axis, f, ends, own, near):
    outer = place(axis)[1]
    zero = jnp.zeros_like(ends[0])
    mine = oriented(axis, ends, own, f)
    other = oriented(axis, (zero, zero), near, f)
    q1, q2, r1, r2 = pick(outer, other[2:], mine[2:])
    slope = jnp.where(outer, mine[5], other[5])
    step = q2 / (1.0 - q1 * slope)
    part = jnp.where(outer, step * mine[1], mine[1] + step * slope * mine[0])
    return part, r2 + step * slope * r1


def pair_whole(axis, f, ends, near_ends, own, near):
    outer = place(axis)[1]
    mine = oriented(axis, ends, own, f)
    other = oriented(axis, near_ends, near, f)
    first, then = pick(outer, mine, other), pick(outer, other, mine)
    return along(then, (first[1], first[5]))


def pair_values(axis, f, ends, near_ends, own, near, far):
    second, outer, _ = place(axis)
    zero = jnp.zeros_like(ends[0])
    mine = oriented(axis, ends, own, f)
    other = oriented(axis, near_ends, near, f)
    ahead = pick(outer, along(mirrored(other), far), far)
    behind = pick(outer, (zero, zero), (other[1], other[5]))
    back, front = beside(mine, behind, ahead)
    return pick(second, (front, back), (back, front))


def scan_values(axis, f, blocks, ends, own, ports):
    me, n = lax.axis_index(axis), lax.axis_size(axis)
    mine = tuple(ends) + tuple(own[v, f] for v in range(4))
    zero = jnp.zeros_like(mine[0])

    def port_of(j):
        return tuple(ports[j, 2 * f + v] for v in range(2)) + tuple(
            ports[j, 2 * blocks + blocks * v + f] for v in range(4)
        )

    def step(j, sides):
        left, right = sides
        left = pick(j < me, along(port_of(j), left), left)
        i = n - 1 - j
        right = pick(i > me, along(mirrored(port_of(i)), right), right)
        return left, right

    left, right = lax.fori_loop(0, n, step, ((zero, zero), (zero, zero)))
    return beside(mine, left, right)


def everyones(axis, ends, own):
    blocks = own.shape[1]
    return lax.all_gather(
        jnp.concatenate([ends, own.reshape((4 * blocks,) + own.shape[2:])]), axis
    )


def swap(value, axis, k):
    return lax.ppermute(value, axis, [(i, i ^ k) for i in range(lax.axis_size(axis))])


PLANES = ("load", "lat", "up", "cx", "cy", "cz")


def open_kernel(nx, nz, *refs):
    ins, outs, tiles, sems = refs[:8], refs[8:16], refs[16], refs[17]
    copies = [pltpu.make_async_copy(a, b, sems.at[i]) for i, (a, b) in enumerate(zip(ins, outs))]
    for copy in copies:
        copy.start()
    upper = lax.axis_index("gz")
    edge, inner = 1 - upper, 2 - 3 * upper
    planes = [(0, edge), (1, edge), (0, inner), (1, inner)] + [(i, edge) for i in range(2, 8)]
    per_tile = nz // nx
    arrived = set()
    lane = lax.broadcasted_iota(jnp.int32, outs[0].shape[1:], 1)
    for first in range(0, len(planes), per_tile):
        tile = None
        for a, (i, offset) in enumerate(planes[first : first + per_tile]):
            if i not in arrived:
                copies[i].wait()
                arrived.add(i)
            plane = None
            for k in range(nx):
                to = nx * a + k
                moved = pltpu.roll(outs[i][k], lax.rem(offset + (to + nz), nz), 1)
                plane = moved if k == 0 else jnp.where(lane == to, moved, plane)
            tile = plane if a == 0 else jnp.where(lane < nx * a, tile, plane)
        tiles[first // per_tile] = tile


def put(ref, f):
    def store(k, v):
        ref[f, k] = v

    return store


def coef_kernel(nx, ny, t, h, lat, cx, cy, xi, xm, xu, xq, xr, yi, ym, yu, yq, yr, xown, yown, one, two):
    even = lax.axis_index("gy") % 2 == 0
    for f, (ratio, ref) in enumerate(zip(RATIOS, (t, h))):
        low = ref[pl.ds(0, nx, stride=ny), :]
        high = ref[pl.ds(ny - 1, nx, stride=ny), :]
        one[f] = jnp.where(even, high, low)
        two[f] = jnp.where(even, low, high)
    for f, ratio in enumerate(RATIOS):
        own = factor(
            nx,
            lambda k: lat[pl.ds(k * ny, ny), :],
            lambda k: 0.5 * cx[pl.ds(k * ny, ny), :],
            ratio,
            *(put(ref, f) for ref in (xi, xm, xu, xq, xr)),
        )
        for v in range(4):
            xown[v, f] = own[v]
        own = factor(
            ny,
            lambda k: lat[pl.ds(k, nx, stride=ny), :],
            lambda k: 0.5 * cy[pl.ds(k, nx, stride=ny), :],
            ratio,
            *(put(ref, f) for ref in (yi, ym, yu, yq, yr)),
        )
        for v in range(4):
            yown[v, f] = own[v]


class Ghost:
    def __init__(self, shape, nx):
        self.shape, self.nx = shape, nx
        self.first = lax.broadcasted_iota(jnp.int32, shape, 1) < shape[1] // 2
        self.ratio = jnp.where(self.first, RATIOS[0], RATIOS[1])

    def lane(self, tiles, plane, k):
        at = self.nx * plane + k
        column = tiles[at // self.shape[1], :, at % self.shape[1] : at % self.shape[1] + 1]
        return jnp.broadcast_to(column, self.shape)

    def fields(self, tiles, plane, k):
        return jnp.where(self.first, self.lane(tiles, plane, k), self.lane(tiles, plane + 1, k))

    def named(self, tiles, name, k):
        return self.lane(tiles, 4 + PLANES.index(name), k)


def lateral_step(v, lateral, half):
    ny = v.shape[0]
    me, n = lax.axis_index("gy"), lax.axis_size("gy")
    row = lax.broadcasted_iota(jnp.int32, v.shape, 0)
    ahead = jnp.where(row == ny - 1, 0.0, pltpu.roll(v, ny - 1, 0))
    behind = jnp.where(row == 0, 0.0, pltpu.roll(v, 1, 0))
    east, west = lateral - half, lateral + half
    inside_high = (row == ny - 1) & (me < n - 1)
    inside_low = (row == 0) & (me > 0)
    side = jnp.where(inside_high, east, jnp.where(inside_low, west, 0.0))
    return east * (ahead - v) + west * (behind - v), side


def vertical_step(nz, v, column, lateral, half):
    upper = lax.axis_index("gz")
    lane = lax.broadcasted_iota(jnp.int32, v.shape, 1)
    column = jnp.broadcast_to(column, v.shape)
    ahead = jnp.where(lane == nz - 1, jnp.where(upper == 0, column, 0.0), pltpu.roll(v, nz - 1, 1))
    behind = jnp.where(lane == 0, jnp.where(upper == 0, 0.0, column), pltpu.roll(v, 1, 1))
    return (lateral - half) * (ahead - v) + (lateral + half) * (behind - v)


def early_kernel(
    nx, nz, t, h, load, lat, up, cy, cz, mine, tiles, xown,
    gi, gm, gu, gq, gr, own, d, side, gd, gside,
):
    upper = lax.axis_index("gz")
    ghost = Ghost(tiles.shape[1:], nx)

    def keep(ref):
        def store(k, v):
            ref[k] = v

        return store

    lateral = [ghost.ratio * ghost.named(tiles, "lat", k) for k in range(nx)]
    ports = factor(
        nx,
        lambda k: lateral[k],
        lambda k: 0.5 * ghost.named(tiles, "cx", k),
        1.0,
        *(keep(ref) for ref in (gi, gm, gu, gq, gr)),
    )
    for v in range(4):
        own[v, 0] = xown[v, 0]
        own[v, 1] = xown[v, 1]
        own[v, 2] = ports[v]
    for k in range(nx):
        v = ghost.fields(tiles, 0, k)
        step, gside[k] = lateral_step(v, lateral[k], 0.5 * ghost.named(tiles, "cy", k))
        inner, here = ghost.fields(tiles, 2, k), ghost.fields(mine, 0, k)
        ahead, behind = jnp.where(upper == 0, inner, here), jnp.where(upper == 0, here, inner)
        rise, half = ghost.ratio * ghost.named(tiles, "up", k), 0.5 * ghost.named(tiles, "cz", k)
        step = step + ((rise - half) * (ahead - v) + (rise + half) * (behind - v))
        gd[k] = v + step + jnp.where(ghost.first, ghost.named(tiles, "load", k), 0.0)
    for f, (ratio, ref) in enumerate(zip(RATIOS, (t, h))):
        for k in range(nx):
            v = ref[k]
            step, side[f, k] = lateral_step(v, ratio * lat[k], 0.5 * cy[k])
            at = nx * f + k
            out = v + step + vertical_step(
                nz, v, tiles[0, :, at : at + 1], ratio * up[k], 0.5 * cz[k]
            )
            d[f, k] = out + load[k] if f == 0 else out


def first_kernel(
    nx, ny, faces, d0, side, gd, gside, xi, xm, xu, gi, gm, gu, d, p, gp, ends
):
    odd = lax.axis_index("gy") % 2
    half = ny // 2
    for f in range(2):
        for k in range(nx):
            low = faces[1 - odd, f, pl.ds(k, half, stride=0), :]
            high = faces[odd, f, pl.ds(k, half, stride=0), :]
            d[f, k, :half] = d0[f, k, :half] + side[f, k, :half] * low
            d[f, k, half:] = d0[f, k, half:] + side[f, k, half:] * high
        ends[2 * f], ends[2 * f + 1] = sweep(
            nx, lambda k: d[f, k], lambda k: xi[f, k], lambda k: xm[f, k], lambda k: xu[f, k], put(p, f)
        )
    low_row = faces[1 - odd, 2, pl.ds(ny - 1, half, stride=0), :]
    high_row = faces[odd, 2, pl.ds(0, half, stride=0), :]
    first = lax.broadcasted_iota(jnp.int32, low_row.shape, 1) < low_row.shape[1] // 2

    def spread(row, k):
        a = jnp.broadcast_to(row[:, k : k + 1], row.shape)
        b = jnp.broadcast_to(row[:, nx + k : nx + k + 1], row.shape)
        return jnp.where(first, a, b)

    def rhs(k):
        beside_rows = jnp.concatenate([spread(low_row, k), spread(high_row, k)])
        return gd[k] + gside[k] * beside_rows

    def keep(k, v):
        gp[k] = v

    ends[4], ends[5] = sweep(
        nx, rhs, lambda k: gi[k], lambda k: gm[k], lambda k: gu[k], keep
    )


def pair_kernel(axis, blocks, ends, near_ends, own, near, out):
    for f in range(blocks):
        source, slope = pair_whole(
            axis, f, (ends[2 * f], ends[2 * f + 1]), (near_ends[2 * f], near_ends[2 * f + 1]), own, near
        )
        if f == 2:
            lane = lax.broadcasted_iota(jnp.int32, source.shape, 1)
            out[4] = jnp.where((lane & 32) == 0, source, slope)
        else:
            out[2 * f] = source
            out[2 * f + 1] = slope


def far_word(far, f):
    if f < 2:
        return far[2 * f], far[2 * f + 1]
    both = far[4]
    lane = lax.broadcasted_iota(jnp.int32, both.shape, 1)
    source = jnp.where((lane & 32) == 0, both, pltpu.roll(both, 32, 1))
    slope = jnp.where((lane & 32) == 0, pltpu.roll(both, both.shape[1] - 32, 1), both)
    return source, slope


def second_kernel(
    paired, nx, ny, nz, p, q, r, gp, gq, gr, ends, near_ends, own, near, far,
    d, load, up, cz, yi, ym, yu, yown, ynear, py, *rest,
):
    outs, s = rest[:-1], rest[-1]

    def values(f):
        mine = (ends[2 * f], ends[2 * f + 1])
        if not paired[0]:
            return scan_values("gx", f, 3, mine, own, far)
        other = (near_ends[2 * f], near_ends[2 * f + 1])
        return pair_values("gx", f, mine, other, own, near, far_word(far, f))

    ghost_low, ghost_high = values(2)
    slopes = []
    for f, ratio in enumerate(RATIOS):
        low, high = values(f)
        for k in range(nx):
            v = p[f, k] + q[f, k] * low + r[f, k] * high
            beyond = gp[k] + gq[k] * ghost_low + gr[k] * ghost_high
            at = f * nz // 2
            out = 2.0 * v - d[f, k]
            out = out + vertical_step(nz, v, beyond[:, at : at + 1], ratio * up[k], 0.5 * cz[k])
            if f == 0:
                out = out + load[k]
            s[f, pl.ds(k * ny, ny), :] = out
        mine = sweep(
            ny,
            lambda k: s[f, pl.ds(k, nx, stride=ny), :],
            lambda k: yi[f, k],
            lambda k: ym[f, k],
            lambda k: yu[f, k],
            put(py, f),
        )
        outs[0][2 * f], outs[0][2 * f + 1] = mine
        if paired[1]:
            outs[1][f], slope = pair_source("gy", f, mine, yown, ynear)
            slopes.append(slope)
    if paired[1]:
        outs[1][2] = jnp.where(place("gy")[2] == 0, slopes[0], slopes[1])


def new_kernel(paired, nx, ny, p, q, r, ends, near_ends, own, near, *rest):
    received, news = rest[:-2], rest[-2:]
    for f, ref in enumerate(news):
        mine = (ends[2 * f], ends[2 * f + 1])
        if paired:
            other = (near_ends[2 * f], near_ends[2 * f + 1])
            two, three = received
            slope = jnp.where(place("gy")[2] == f, two[2], three[2])
            low, high = pair_values("gy", f, mine, other, own, near, (two[f] + three[f], slope))
        else:
            low, high = scan_values("gy", f, 2, mine, own, received[0])
        for k in range(ny):
            ref[pl.ds(k, nx, stride=ny), :] = p[f, k] + q[f, k] * low + r[f, k] * high


def neighbours(one, two):
    across, n = lax.axis_size("gx"), lax.axis_size("gy")

    def swapped(first, value):
        partner = {i: i ^ 1 if first == 0 else ((i + 1) ^ 1) - 1 for i in range(n)}
        pairs = []
        for x in range(across):
            for i in range(n):
                j = partner[i]
                target = (x, j) if 0 <= j < n else (x ^ 1, i)
                if target[0] < across:
                    pairs.append((x * n + i, target[0] * n + target[1]))
        return lax.ppermute(value, ("gx", "gy"), pairs)

    return swapped(0, one), swapped(1, two)


def body(thermal, vapour, load, lat, up, cx, cy, cz):
    nx, ny, nz = thermal.shape
    assert lax.axis_size("gz") == 2 and nx * 8 == nz
    flat = (nx * ny, nz)
    lines_x, lines_y = (2, nx, ny, nz), (2, ny, nx, nz)
    block_x, block_y = (ny, nz), (nx, nz)
    paired = (lax.axis_size("gx") == 4, lax.axis_size("gy") == 4)
    thermal, vapour, load, lat, up, cx, cy, cz, mine = call(
        functools.partial(open_kernel, nx, nz),
        (thermal.shape,) * 8 + ((2,) + block_x,),
        *(
            pltpu.with_memory_space_constraint(a, pltpu.HBM)
            for a in (thermal, vapour, load, lat, up, cx, cy, cz)
        ),
        scratch=[pltpu.SemaphoreType.DMA((8,))],
        space=pltpu.HBM,
    )
    tiles = swap(mine, "gz", 1)
    xi, xm, xu, xq, xr, yi, ym, yu, yq, yr, xown, yown, one, two = call(
        functools.partial(coef_kernel, nx, ny),
        (lines_x,) * 5
        + (lines_y,) * 5
        + ((4, 2) + block_x, (4, 2) + block_y, (2,) + block_y, (2,) + block_y),
        *(a.reshape(flat) for a in (thermal, vapour, lat, cx, cy)),
    )
    one, two = neighbours(
        jnp.concatenate([one, tiles[:1]]), jnp.concatenate([two, tiles[:1]])
    )
    gi, gm, gu, gq, gr, own, d, side, gd, gside = call(
        functools.partial(early_kernel, nx, nz),
        ((nx,) + block_x,) * 5 + ((4, 3) + block_x, lines_x, lines_x) + ((nx,) + block_x,) * 2,
        thermal, vapour, load, lat, up, cy, cz, mine, tiles, xown,
    )
    near = swap(own, "gx", 1) if paired[0] else own
    ynear = swap(yown, "gy", 1) if paired[1] else yown
    d, p, gp, ends = call(
        functools.partial(first_kernel, nx, ny),
        (lines_x, lines_x, (nx,) + block_x, (6,) + block_x),
        jnp.stack([one, two]), d, side, gd, gside, xi, xm, xu, gi, gm, gu,
    )
    if paired[0]:
        near_ends = swap(ends, "gx", 1)
        (word,) = call(functools.partial(pair_kernel, "gx", 3), ((5,) + block_x,), ends, near_ends, own, near)
        far = swap(word, "gx", 2)
    else:
        near_ends, far = ends, everyones("gx", ends, own)
    py, yends, *outs = call(
        functools.partial(second_kernel, paired, nx, ny, nz),
        (lines_y, (4,) + block_y) + (((3,) + block_y,) if paired[1] else ()),
        p, xq, xr, gp, gq, gr, ends, near_ends, own, near, far,
        d, load, up, cz, yi, ym, yu, yown, ynear,
        scratch=[pltpu.VMEM((2,) + flat, F32)],
    )
    if paired[1]:
        received = [swap(outs[0], "gy", k) for k in (2, 3)]
        near_ends = swap(yends, "gy", 1)
    else:
        near_ends, received = yends, [everyones("gy", yends, yown)]
    t_new, h_new = call(
        functools.partial(new_kernel, paired[1], nx, ny),
        (flat, flat),
        py, yq, yr, yends, near_ends, yown, ynear, *received,
    )
    return t_new.reshape(thermal.shape), h_new.reshape(thermal.shape)


def solution(mesh):
    spec = P("gx", "gy", "gz")
    return jax.shard_map(body, mesh=mesh, in_specs=(spec,) * 8, out_specs=(spec, spec), check_vma=False)
```

```python
import functools

import jax
import jax.numpy as jnp
from jax import lax
from jax.experimental import pallas as pl
from jax.experimental.pallas import tpu as pltpu
from jax.sharding import PartitionSpec as P


RATIOS = (1.0, 0.8)
F32 = jnp.float32


def vmem():
    return pl.BlockSpec(memory_space=pltpu.VMEM)


def call(kernel, outs, *args, scratch=(), flops=400000, space=pltpu.VMEM):
    size = sum(4 * a.size for a in args)
    return run(kernel, outs, args, scratch, flops, size, space)


def run(kernel, outs, args, scratch, flops, size, space):
    return pl.pallas_call(
        kernel,
        out_shape=tuple(jax.ShapeDtypeStruct(s, F32) for s in outs),
        in_specs=[pl.BlockSpec(memory_space=space)] * len(args),
        out_specs=tuple(vmem() for _ in outs),
        scratch_shapes=list(scratch),
        compiler_params=pltpu.CompilerParams(vmem_limit_bytes=8 << 20),
        cost_estimate=pl.CostEstimate(flops=flops, bytes_accessed=size, transcendentals=0),
    )(*args)


def factor(n, lat, half_cfl, ratio, inv_out, mid_out, up_out, first_out, last_out):
    ups, firsts = [], []
    up = first = None
    for k in range(n):
        lateral = ratio * lat(k)
        half = half_cfl(k)
        east, west = lateral - half, lateral + half
        pivot = 1.0 + 2.0 * lateral
        if k:
            pivot = pivot - west * up
        inverse = 1.0 / pivot
        mid = west * inverse
        up = east * inverse
        first = mid if k == 0 else mid * first
        inv_out(k, inverse)
        mid_out(k, mid)
        up_out(k, up)
        ups.append(up)
        firsts.append(first)
    q, r = firsts[-1], ups[-1]
    first_out(n - 1, q)
    last_out(n - 1, r)
    q2, r2 = q, r
    for k in range(n - 2, -1, -1):
        q = firsts[k] + ups[k] * q
        r = ups[k] * r
        first_out(k, q)
        last_out(k, r)
    return q, q2, r, r2


def sweep(n, rhs, inv, mid, up, out):
    values = []
    value = None
    for k in range(n):
        value = inv(k) * rhs(k) if k == 0 else inv(k) * rhs(k) + mid(k) * value
        values.append(value)
    out(n - 1, value)
    last = value
    for k in range(n - 2, -1, -1):
        value = values[k] + up(k) * value
        out(k, value)
    return value, last


def along(port, before):
    p1, p2, q1, q2, r1, r2 = port
    source, slope = before
    t = 1.0 / (1.0 - q1 * slope)
    step = q2 * slope * t
    return p2 + q2 * source + step * (p1 + q1 * source), r2 + step * r1


def mirrored(port):
    p1, p2, q1, q2, r1, r2 = port
    return p2, p1, r2, r1, q2, q1


def pick(flag, a, b):
    return tuple(jnp.where(flag, x, y) for x, y in zip(a, b))


def beside(port, left, right):
    p1, p2, q1, q2, r1, r2 = port
    pl_, ql = left
    pr, qr = right
    a1 = p1 + q1 * pl_ + r1 * pr
    a2 = p2 + q2 * pl_ + r2 * pr
    b11, b22 = 1.0 - q1 * ql, 1.0 - r2 * qr
    b12, b21 = r1 * qr, q2 * ql
    t = 1.0 / (b11 * b22 - b12 * b21)
    u1 = (a1 * b22 + b12 * a2) * t
    u2 = (b11 * a2 + b21 * a1) * t
    return pl_ + ql * u1, pr + qr * u2


def place(axis):
    me = lax.axis_index(axis)
    second = me // 2
    return second == 1, second == me % 2, me % 2


def coefs_of(ref, f):
    return tuple(ref[v, f] for v in range(4))


def oriented(axis, ends, coefs):
    port = tuple(ends) + tuple(coefs)
    return pick(place(axis)[0], mirrored(port), port)


def pair_source(axis, ends, own, near):
    outer = place(axis)[1]
    zero = jnp.zeros_like(own[0])
    mine = oriented(axis, ends or (zero, zero), own)
    other = oriented(axis, (zero, zero), near)
    q1, q2, r1, r2 = pick(outer, other[2:], mine[2:])
    slope = jnp.where(outer, mine[5], other[5])
    step = q2 / (1.0 - q1 * slope)
    part = jnp.where(outer, step * mine[1], mine[1] + step * slope * mine[0])
    return part, r2 + step * slope * r1


def pair_values(axis, ends, near_ends, own, near, far):
    second, outer, _ = place(axis)
    zero = jnp.zeros_like(ends[0])
    mine = oriented(axis, ends, own)
    other = oriented(axis, near_ends, near)
    ahead = pick(outer, along(mirrored(other), far), far)
    behind = pick(outer, (zero, zero), (other[1], other[5]))
    back, front = beside(mine, behind, ahead)
    return pick(second, (front, back), (back, front))


def scan_values(axis, mine, port_of):
    me, n = lax.axis_index(axis), lax.axis_size(axis)
    zero = jnp.zeros_like(mine[0])

    def step(j, sides):
        left, right = sides
        left = pick(j < me, along(port_of(j), left), left)
        i = n - 1 - j
        right = pick(i > me, along(mirrored(port_of(i)), right), right)
        return left, right

    left, right = lax.fori_loop(0, n, step, ((zero, zero), (zero, zero)))
    return beside(mine, left, right)


def everyones(axis, ends, own, *more):
    return lax.all_gather(
        jnp.concatenate([ends, own.reshape((8,) + own.shape[2:]), *more]), axis
    )


def swap(value, axis, k):
    return lax.ppermute(value, axis, [(i, i ^ k) for i in range(lax.axis_size(axis))])


PLANES = ("load", "lat", "up", "cx", "cy", "cz")


def open_kernel(nx, nz, *refs):
    ins, outs, tiles, sems = refs[:8], refs[8:16], refs[16], refs[17]
    copies = [pltpu.make_async_copy(a, b, sems.at[i]) for i, (a, b) in enumerate(zip(ins, outs))]
    for copy in copies:
        copy.start()
    upper = lax.axis_index("gz")
    edge, inner = 1 - upper, 2 - 3 * upper
    planes = [(0, edge), (1, edge), (0, inner), (1, inner)] + [(i, edge) for i in range(2, 8)]
    lane = lax.broadcasted_iota(jnp.int32, outs[0].shape[1:], 1)

    def plane(a, i, offset):
        moved = [
            pltpu.roll(outs[i][k], lax.rem(offset + (nx * a + k + nz), nz), 1) for k in range(nx)
        ]
        bit = 1
        while len(moved) > 1:
            moved = [jnp.where((lane & bit) == 0, x, y) for x, y in zip(moved[::2], moved[1::2])]
            bit *= 2
        return moved[0]

    per_tile = nz // nx
    packed = []
    for group in (range(2), range(2, 8)):
        for i in group:
            copies[i].wait()
        for n, (i, offset) in enumerate(planes):
            if i in group:
                packed.append((n, plane(n % per_tile, i, offset)))
    for first in range(0, len(planes), per_tile):
        tile = None
        for n, part in packed:
            if first <= n < first + per_tile:
                at = nx * (n - first)
                tile = part if tile is None else jnp.where(lane < at, tile, part)
        tiles[first // per_tile] = tile


def put(ref, f):
    def store(k, v):
        ref[f, k] = v

    return store


def coef_kernel(nx, ny, t, h, lat, cx, cy, xi, xm, xu, xq, xr, yi, ym, yu, yq, yr, xown, yown, one, two):
    even = lax.axis_index("gy") % 2 == 0
    for f, (ratio, ref) in enumerate(zip(RATIOS, (t, h))):
        low = ref[pl.ds(0, nx, stride=ny), :]
        high = ref[pl.ds(ny - 1, nx, stride=ny), :]
        one[f] = jnp.where(even, high, low)
        two[f] = jnp.where(even, low, high)
    for f, ratio in enumerate(RATIOS):
        own = factor(
            nx,
            lambda k: lat[pl.ds(k * ny, ny), :],
            lambda k: 0.5 * cx[pl.ds(k * ny, ny), :],
            ratio,
            *(put(ref, f) for ref in (xi, xm, xu, xq, xr)),
        )
        for v in range(4):
            xown[v, f] = own[v]
        own = factor(
            ny,
            lambda k: lat[pl.ds(k, nx, stride=ny), :],
            lambda k: 0.5 * cy[pl.ds(k, nx, stride=ny), :],
            ratio,
            *(put(ref, f) for ref in (yi, ym, yu, yq, yr)),
        )
        for v in range(4):
            yown[v, f] = own[v]


def slope_kernel(axis, own, near, out):
    for f in range(2):
        out[f] = pair_source(axis, None, coefs_of(own, f), coefs_of(near, f))[1]


class Ghost:
    def __init__(self, shape, nx):
        self.shape, self.nx = shape, nx
        self.first = lax.broadcasted_iota(jnp.int32, shape, 1) < shape[1] // 2
        self.ratio = jnp.where(self.first, RATIOS[0], RATIOS[1])

    def lane(self, tiles, plane, k):
        at = self.nx * plane + k
        column = tiles[at // self.shape[1], :, at % self.shape[1] : at % self.shape[1] + 1]
        return jnp.broadcast_to(column, self.shape)

    def fields(self, tiles, plane, k):
        return jnp.where(self.first, self.lane(tiles, plane, k), self.lane(tiles, plane + 1, k))

    def named(self, tiles, name, k):
        return self.lane(tiles, 4 + PLANES.index(name), k)


def lateral_step(v, lateral, half):
    ny = v.shape[0]
    me, n = lax.axis_index("gy"), lax.axis_size("gy")
    row = lax.broadcasted_iota(jnp.int32, v.shape, 0)
    ahead = jnp.where(row == ny - 1, 0.0, pltpu.roll(v, ny - 1, 0))
    behind = jnp.where(row == 0, 0.0, pltpu.roll(v, 1, 0))
    east, west = lateral - half, lateral + half
    inside_high = (row == ny - 1) & (me < n - 1)
    inside_low = (row == 0) & (me > 0)
    side = jnp.where(inside_high, east, jnp.where(inside_low, west, 0.0))
    return east * (ahead - v) + west * (behind - v), side


def vertical_step(nz, v, column, lateral, half):
    upper = lax.axis_index("gz")
    lane = lax.broadcasted_iota(jnp.int32, v.shape, 1)
    column = jnp.broadcast_to(column, v.shape)
    ahead = jnp.where(lane == nz - 1, jnp.where(upper == 0, column, 0.0), pltpu.roll(v, nz - 1, 1))
    behind = jnp.where(lane == 0, jnp.where(upper == 0, 0.0, column), pltpu.roll(v, 1, 1))
    return (lateral - half) * (ahead - v) + (lateral + half) * (behind - v)


def ghost_kernel(nx, tiles, gi, gm, gu, gq, gr, own):
    ghost = Ghost(tiles.shape[1:], nx)

    def keep(ref):
        def store(k, v):
            ref[k] = v

        return store

    ports = factor(
        nx,
        lambda k: ghost.named(tiles, "lat", k),
        lambda k: 0.5 * ghost.named(tiles, "cx", k),
        ghost.ratio,
        *(keep(ref) for ref in (gi, gm, gu, gq, gr)),
    )
    for v in range(4):
        own[v] = ports[v]


def early_kernel(
    nx, nz, t, h, load, lat, up, cy, cz, mine, tiles, d, side, gd, gside
):
    upper = lax.axis_index("gz")
    ghost = Ghost(tiles.shape[1:], nx)
    for k in range(nx):
        v = ghost.fields(tiles, 0, k)
        lateral = ghost.ratio * ghost.named(tiles, "lat", k)
        step, gside[k] = lateral_step(v, lateral, 0.5 * ghost.named(tiles, "cy", k))
        inner, here = ghost.fields(tiles, 2, k), ghost.fields(mine, 0, k)
        ahead, behind = jnp.where(upper == 0, inner, here), jnp.where(upper == 0, here, inner)
        rise, half = ghost.ratio * ghost.named(tiles, "up", k), 0.5 * ghost.named(tiles, "cz", k)
        step = step + ((rise - half) * (ahead - v) + (rise + half) * (behind - v))
        gd[k] = v + step + jnp.where(ghost.first, ghost.named(tiles, "load", k), 0.0)
    for f, (ratio, ref) in enumerate(zip(RATIOS, (t, h))):
        for k in range(nx):
            v = ref[k]
            step, side[f, k] = lateral_step(v, ratio * lat[k], 0.5 * cy[k])
            at = nx * f + k
            out = v + step + vertical_step(
                nz, v, tiles[0, :, at : at + 1], ratio * up[k], 0.5 * cz[k]
            )
            d[f, k] = out + load[k] if f == 0 else out


def first_kernel(
    paired, nx, ny, faces, d0, side, gd, gside, xi, xm, xu, gi, gm, gu, own, near, gown, gnear,
    d, p, gp, ends, *word
):
    odd = lax.axis_index("gy") % 2
    half = ny // 2
    for f in range(2):
        for k in range(nx):
            low = faces[1 - odd, f, pl.ds(k, half, stride=0), :]
            high = faces[odd, f, pl.ds(k, half, stride=0), :]
            d[f, k, :half] = d0[f, k, :half] + side[f, k, :half] * low
            d[f, k, half:] = d0[f, k, half:] + side[f, k, half:] * high
        mine = sweep(
            nx, lambda k: d[f, k], lambda k: xi[f, k], lambda k: xm[f, k], lambda k: xu[f, k], put(p, f)
        )
        ends[2 * f], ends[2 * f + 1] = mine
        if paired:
            word[0][f] = pair_source("gx", mine, coefs_of(own, f), coefs_of(near, f))[0]
    low_row = faces[1 - odd, 2, pl.ds(ny - 1, half, stride=0), :]
    high_row = faces[odd, 2, pl.ds(0, half, stride=0), :]
    first = lax.broadcasted_iota(jnp.int32, low_row.shape, 1) < low_row.shape[1] // 2

    def spread(row, k):
        a = jnp.broadcast_to(row[:, k : k + 1], row.shape)
        b = jnp.broadcast_to(row[:, nx + k : nx + k + 1], row.shape)
        return jnp.where(first, a, b)

    def rhs(k):
        beside_rows = jnp.concatenate([spread(low_row, k), spread(high_row, k)])
        return gd[k] + gside[k] * beside_rows

    def keep(k, v):
        gp[k] = v

    mine = sweep(nx, rhs, lambda k: gi[k], lambda k: gm[k], lambda k: gu[k], keep)
    ends[4] = packed(*mine)
    if paired:
        word[0][2] = packed(*pair_source("gx", mine, x_coefs(own, gown, 2), x_coefs(near, gnear, 2)))


def packed(a, b):
    lane = lax.broadcasted_iota(jnp.int32, a.shape, 1)
    return jnp.where((lane & 32) == 0, a, b)


def unpacked(both):
    lane = lax.broadcasted_iota(jnp.int32, both.shape, 1)
    a = jnp.where((lane & 32) == 0, both, pltpu.roll(both, 32, 1))
    b = jnp.where((lane & 32) == 0, pltpu.roll(both, both.shape[1] - 32, 1), both)
    return a, b


def x_ends(ends, f):
    return (ends[2 * f], ends[2 * f + 1]) if f < 2 else unpacked(ends[4])


def x_coefs(own, ghost, f):
    return coefs_of(own, f) if f < 2 else tuple(ghost[v] for v in range(4))


def second_kernel(
    paired, nx, ny, nz, p, q, r, gp, gq, gr, ends, near_ends, own, near, gown, gnear, slopes,
    d, load, up, cz, yi, ym, yu, yown, ynear, *rest,
):
    far, (py, *outs, s) = rest[: 1 + paired[0]], rest[1 + paired[0] :]

    def values(f):
        mine, coefs = x_ends(ends, f), x_coefs(own, gown, f)
        if paired[0]:
            two, three = far
            if f < 2:
                word = two[f] + three[f], slopes[f]
            else:
                word, more = unpacked(two[2]), unpacked(three[2])
                word = word[0] + more[0], word[1]
            other, other_coefs = x_ends(near_ends, f), x_coefs(near, gnear, f)
            return pair_values("gx", mine, other, coefs, other_coefs, word)

        def port_of(j):
            theirs = x_ends(far[0].at[j], f)
            at = [5 + 2 * v + f if f < 2 else 13 + v for v in range(4)]
            return tuple(theirs) + tuple(far[0][j, i] for i in at)

        return scan_values("gx", tuple(mine) + coefs, port_of)

    ghost_low, ghost_high = values(2)
    for f, ratio in enumerate(RATIOS):
        low, high = values(f)
        for k in range(nx):
            v = p[f, k] + q[f, k] * low + r[f, k] * high
            beyond = gp[k] + gq[k] * ghost_low + gr[k] * ghost_high
            at = f * nz // 2
            out = 2.0 * v - d[f, k]
            out = out + vertical_step(nz, v, beyond[:, at : at + 1], ratio * up[k], 0.5 * cz[k])
            if f == 0:
                out = out + load[k]
            s[f, pl.ds(k * ny, ny), :] = out
        mine = sweep(
            ny,
            lambda k: s[f, pl.ds(k, nx, stride=ny), :],
            lambda k: yi[f, k],
            lambda k: ym[f, k],
            lambda k: yu[f, k],
            put(py, f),
        )
        outs[0][2 * f], outs[0][2 * f + 1] = mine
        if paired[1]:
            outs[1][f] = pair_source("gy", mine, coefs_of(yown, f), coefs_of(ynear, f))[0]


def new_kernel(paired, nx, ny, p, q, r, ends, near_ends, own, near, slopes, *rest):
    received, news = rest[:-2], rest[-2:]
    for f, ref in enumerate(news):
        mine = (ends[2 * f], ends[2 * f + 1])
        coefs = coefs_of(own, f)
        if paired:
            other = (near_ends[2 * f], near_ends[2 * f + 1])
            two, three = received
            low, high = pair_values(
                "gy", mine, other, coefs, coefs_of(near, f), (two[f] + three[f], slopes[f])
            )
        else:
            (ports,) = received

            def port_of(j):
                return (ports[j, 2 * f], ports[j, 2 * f + 1]) + tuple(
                    ports[j, 4 + 2 * v + f] for v in range(4)
                )

            low, high = scan_values("gy", mine + coefs, port_of)
        for k in range(ny):
            ref[pl.ds(k, nx, stride=ny), :] = p[f, k] + q[f, k] * low + r[f, k] * high


def neighbours(one, two):
    across, n = lax.axis_size("gx"), lax.axis_size("gy")

    def swapped(first, value):
        partner = {i: i ^ 1 if first == 0 else ((i + 1) ^ 1) - 1 for i in range(n)}
        pairs = []
        for x in range(across):
            for i in range(n):
                j = partner[i]
                target = (x, j) if 0 <= j < n else (x ^ 1, i)
                if target[0] < across:
                    pairs.append((x * n + i, target[0] * n + target[1]))
        return lax.ppermute(value, ("gx", "gy"), pairs)

    return swapped(0, one), swapped(1, two)


def body(thermal, vapour, load, lat, up, cx, cy, cz):
    nx, ny, nz = thermal.shape
    assert lax.axis_size("gz") == 2 and nx * 8 == nz
    flat = (nx * ny, nz)
    lines_x, lines_y = (2, nx, ny, nz), (2, ny, nx, nz)
    block_x, block_y = (ny, nz), (nx, nz)
    paired = (lax.axis_size("gx") == 4, lax.axis_size("gy") == 4)
    thermal, vapour, load, lat, up, cx, cy, cz, mine = call(
        functools.partial(open_kernel, nx, nz),
        (thermal.shape,) * 8 + ((2,) + block_x,),
        *(
            pltpu.with_memory_space_constraint(a, pltpu.HBM)
            for a in (thermal, vapour, load, lat, up, cx, cy, cz)
        ),
        scratch=[pltpu.SemaphoreType.DMA((8,))],
        space=pltpu.HBM,
    )
    tiles = swap(mine, "gz", 1)
    xi, xm, xu, xq, xr, yi, ym, yu, yq, yr, xown, yown, one, two = call(
        functools.partial(coef_kernel, nx, ny),
        (lines_x,) * 5
        + (lines_y,) * 5
        + ((4, 2) + block_x, (4, 2) + block_y, (2,) + block_y, (2,) + block_y),
        *(a.reshape(flat) for a in (thermal, vapour, lat, cx, cy)),
    )
    xnear, ynear, xslopes, yslopes = xown, yown, xown[0], yown[0]
    if paired[0]:
        xnear = swap(xown, "gx", 1)
        (xslopes,) = call(functools.partial(slope_kernel, "gx"), ((2,) + block_x,), xown, xnear)
        xslopes = swap(xslopes, "gx", 2)
    if paired[1]:
        ynear = swap(yown, "gy", 1)
        (yslopes,) = call(functools.partial(slope_kernel, "gy"), ((2,) + block_y,), yown, ynear)
        yslopes = swap(yslopes, "gy", 3)
    one, two = neighbours(
        jnp.concatenate([one, tiles[:1]]), jnp.concatenate([two, tiles[:1]])
    )
    gi, gm, gu, gq, gr, gown = call(
        functools.partial(ghost_kernel, nx), ((nx,) + block_x,) * 5 + ((4,) + block_x,), tiles
    )
    d, side, gd, gside = call(
        functools.partial(early_kernel, nx, nz),
        (lines_x, lines_x) + ((nx,) + block_x,) * 2,
        thermal, vapour, load, lat, up, cy, cz, mine, tiles,
    )
    gnear = swap(gown, "gx", 1) if paired[0] else gown
    d, p, gp, ends, *word = call(
        functools.partial(first_kernel, paired[0], nx, ny),
        (lines_x, lines_x, (nx,) + block_x, (5,) + block_x) + ((3,) + block_x,) * paired[0],
        jnp.stack([one, two]), d, side, gd, gside, xi, xm, xu, gi, gm, gu, xown, xnear, gown, gnear,
    )
    if paired[0]:
        near_ends = swap(ends, "gx", 1)
        far = [swap(word[0], "gx", k) for k in (2, 3)]
    else:
        near_ends, far = ends, [everyones("gx", ends, xown, gown)]
    py, yends, *outs = call(
        functools.partial(second_kernel, paired, nx, ny, nz),
        (lines_y, (4,) + block_y) + (((2,) + block_y,) if paired[1] else ()),
        p, xq, xr, gp, gq, gr, ends, near_ends, xown, xnear, gown, gnear, xslopes,
        d, load, up, cz, yi, ym, yu, yown, ynear, *far,
        scratch=[pltpu.VMEM((2,) + flat, F32)],
    )
    if paired[1]:
        received = [swap(outs[0], "gy", k) for k in (2, 3)]
        near_ends = swap(yends, "gy", 1)
    else:
        near_ends, received = yends, [everyones("gy", yends, yown)]
    t_new, h_new = call(
        functools.partial(new_kernel, paired[1], nx, ny),
        (flat, flat),
        py, yq, yr, yends, near_ends, yown, ynear, yslopes, *received,
    )
    return t_new.reshape(thermal.shape), h_new.reshape(thermal.shape)


def solution(mesh):
    spec = P("gx", "gy", "gz")
    return jax.shard_map(
        body, mesh=mesh, in_specs=(spec,) * 8, out_specs=(spec, spec), check_vma=False
    )
```

```python
import functools

import jax
import jax.numpy as jnp
from jax import lax
from jax.experimental import pallas as pl
from jax.experimental.pallas import tpu as pltpu
from jax.sharding import PartitionSpec as P


RATIOS = (1.0, 0.8)
F32 = jnp.float32


def vmem():
    return pl.BlockSpec(memory_space=pltpu.VMEM)


def call(kernel, outs, *args, scratch=(), flops=400000, space=pltpu.VMEM):
    size = sum(4 * a.size for a in args)
    return run(kernel, outs, args, scratch, flops, size, space)


def run(kernel, outs, args, scratch, flops, size, space):
    return pl.pallas_call(
        kernel,
        out_shape=tuple(jax.ShapeDtypeStruct(s, F32) for s in outs),
        in_specs=[pl.BlockSpec(memory_space=space)] * len(args),
        out_specs=tuple(vmem() for _ in outs),
        scratch_shapes=list(scratch),
        compiler_params=pltpu.CompilerParams(vmem_limit_bytes=8 << 20),
        cost_estimate=pl.CostEstimate(flops=flops, bytes_accessed=size, transcendentals=0),
    )(*args)


def factor(n, lat, half_cfl, ratio, inv_out, mid_out, up_out, first_out, last_out):
    ups, firsts = [], []
    up = first = None
    for k in range(n):
        lateral = ratio * lat(k)
        half = half_cfl(k)
        east, west = lateral - half, lateral + half
        pivot = 1.0 + 2.0 * lateral
        if k:
            pivot = pivot - west * up
        inverse = 1.0 / pivot
        mid = west * inverse
        up = east * inverse
        first = mid if k == 0 else mid * first
        inv_out(k, inverse)
        mid_out(k, mid)
        up_out(k, up)
        ups.append(up)
        firsts.append(first)
    q, r = firsts[-1], ups[-1]
    first_out(n - 1, q)
    last_out(n - 1, r)
    q2, r2 = q, r
    for k in range(n - 2, -1, -1):
        q = firsts[k] + ups[k] * q
        r = ups[k] * r
        first_out(k, q)
        last_out(k, r)
    return q, q2, r, r2


def sweep(n, rhs, inv, mid, up, out):
    values = []
    value = None
    for k in range(n):
        value = inv(k) * rhs(k) if k == 0 else inv(k) * rhs(k) + mid(k) * value
        values.append(value)
    out(n - 1, value)
    last = value
    for k in range(n - 2, -1, -1):
        value = values[k] + up(k) * value
        out(k, value)
    return value, last


def along(port, before):
    p1, p2, q1, q2, r1, r2 = port
    source, slope = before
    t = 1.0 / (1.0 - q1 * slope)
    step = q2 * slope * t
    return p2 + q2 * source + step * (p1 + q1 * source), r2 + step * r1


def mirrored(port):
    p1, p2, q1, q2, r1, r2 = port
    return p2, p1, r2, r1, q2, q1


def pick(flag, a, b):
    return tuple(jnp.where(flag, x, y) for x, y in zip(a, b))


def beside(port, left, right):
    p1, p2, q1, q2, r1, r2 = port
    pl_, ql = left
    pr, qr = right
    a1 = p1 + q1 * pl_ + r1 * pr
    a2 = p2 + q2 * pl_ + r2 * pr
    b11, b22 = 1.0 - q1 * ql, 1.0 - r2 * qr
    b12, b21 = r1 * qr, q2 * ql
    t = 1.0 / (b11 * b22 - b12 * b21)
    u1 = (a1 * b22 + b12 * a2) * t
    u2 = (b11 * a2 + b21 * a1) * t
    return pl_ + ql * u1, pr + qr * u2


def place(axis):
    me = lax.axis_index(axis)
    second = me // 2
    return second == 1, second == me % 2, me % 2


def coefs_of(ref, f):
    return tuple(ref[v, f] for v in range(4))


def oriented(axis, ends, coefs):
    port = tuple(ends) + tuple(coefs)
    return pick(place(axis)[0], mirrored(port), port)


def pair_source(axis, ends, own, near):
    outer = place(axis)[1]
    zero = jnp.zeros_like(own[0])
    mine = oriented(axis, ends or (zero, zero), own)
    other = oriented(axis, (zero, zero), near)
    q1, q2, r1, r2 = pick(outer, other[2:], mine[2:])
    slope = jnp.where(outer, mine[5], other[5])
    step = q2 / (1.0 - q1 * slope)
    part = jnp.where(outer, step * mine[1], mine[1] + step * slope * mine[0])
    return part, r2 + step * slope * r1


def pair_values(axis, ends, near_ends, own, near, far):
    second, outer, _ = place(axis)
    zero = jnp.zeros_like(ends[0])
    mine = oriented(axis, ends, own)
    other = oriented(axis, near_ends, near)
    ahead = pick(outer, along(mirrored(other), far), far)
    behind = pick(outer, (zero, zero), (other[1], other[5]))
    back, front = beside(mine, behind, ahead)
    return pick(second, (front, back), (back, front))


def scan_values(axis, mine, port_of):
    me, n = lax.axis_index(axis), lax.axis_size(axis)
    zero = jnp.zeros_like(mine[0])

    def step(j, sides):
        left, right = sides
        left = pick(j < me, along(port_of(j), left), left)
        i = n - 1 - j
        right = pick(i > me, along(mirrored(port_of(i)), right), right)
        return left, right

    left, right = lax.fori_loop(0, n, step, ((zero, zero), (zero, zero)))
    return beside(mine, left, right)


def everyones(axis, ends, own, *more):
    return lax.all_gather(
        jnp.concatenate([ends, own.reshape((8,) + own.shape[2:]), *more]), axis
    )


def swap(value, axis, k):
    return lax.ppermute(value, axis, [(i, i ^ k) for i in range(lax.axis_size(axis))])


PLANES = ("load", "lat", "up", "cx", "cy", "cz")


def open_kernel(nx, nz, *refs):
    ins, outs, tiles, sems = refs[:8], refs[8:16], refs[16], refs[17]
    copies = [pltpu.make_async_copy(a, b, sems.at[i]) for i, (a, b) in enumerate(zip(ins, outs))]
    for copy in copies:
        copy.start()
    upper = lax.axis_index("gz")
    edge, inner = 1 - upper, 2 - 3 * upper
    planes = [(0, edge), (1, edge), (0, inner), (1, inner)] + [(i, edge) for i in range(2, 8)]
    lane = lax.broadcasted_iota(jnp.int32, outs[0].shape[1:], 1)

    def plane(a, i, offset):
        moved = [
            pltpu.roll(outs[i][k], lax.rem(offset + (nx * a + k + nz), nz), 1) for k in range(nx)
        ]
        bit = 1
        while len(moved) > 1:
            moved = [jnp.where((lane & bit) == 0, x, y) for x, y in zip(moved[::2], moved[1::2])]
            bit *= 2
        return moved[0]

    per_tile = nz // nx
    packed = []
    for group in (range(2), range(2, 8)):
        for i in group:
            copies[i].wait()
        for n, (i, offset) in enumerate(planes):
            if i in group:
                packed.append((n, plane(n % per_tile, i, offset)))
    for first in range(0, len(planes), per_tile):
        tile = None
        for n, part in packed:
            if first <= n < first + per_tile:
                at = nx * (n - first)
                tile = part if tile is None else jnp.where(lane < at, tile, part)
        tiles[first // per_tile] = tile


def put(ref, f):
    def store(k, v):
        ref[f, k] = v

    return store


def coef_kernel(nx, ny, t, h, lat, cx, cy, xi, xm, xu, xq, xr, yi, ym, yu, yq, yr, xown, yown, one, two):
    even = lax.axis_index("gy") % 2 == 0
    for f, (ratio, ref) in enumerate(zip(RATIOS, (t, h))):
        low = ref[pl.ds(0, nx, stride=ny), :]
        high = ref[pl.ds(ny - 1, nx, stride=ny), :]
        one[f] = jnp.where(even, high, low)
        two[f] = jnp.where(even, low, high)
    for f, ratio in enumerate(RATIOS):
        own = factor(
            nx,
            lambda k: lat[pl.ds(k * ny, ny), :],
            lambda k: 0.5 * cx[pl.ds(k * ny, ny), :],
            ratio,
            *(put(ref, f) for ref in (xi, xm, xu, xq, xr)),
        )
        for v in range(4):
            xown[v, f] = own[v]
        own = factor(
            ny,
            lambda k: lat[pl.ds(k, nx, stride=ny), :],
            lambda k: 0.5 * cy[pl.ds(k, nx, stride=ny), :],
            ratio,
            *(put(ref, f) for ref in (yi, ym, yu, yq, yr)),
        )
        for v in range(4):
            yown[v, f] = own[v]


def slope_kernel(axis, own, near, out):
    for f in range(2):
        out[f] = pair_source(axis, None, coefs_of(own, f), coefs_of(near, f))[1]


class Ghost:
    def __init__(self, shape, nx):
        self.shape, self.nx = shape, nx
        self.first = lax.broadcasted_iota(jnp.int32, shape, 1) < shape[1] // 2
        self.ratio = jnp.where(self.first, RATIOS[0], RATIOS[1])

    def lane(self, tiles, plane, k):
        at = self.nx * plane + k
        column = tiles[at // self.shape[1], :, at % self.shape[1] : at % self.shape[1] + 1]
        return jnp.broadcast_to(column, self.shape)

    def fields(self, tiles, plane, k):
        return jnp.where(self.first, self.lane(tiles, plane, k), self.lane(tiles, plane + 1, k))

    def named(self, tiles, name, k):
        return self.lane(tiles, 4 + PLANES.index(name), k)


def lateral_step(v, lateral, half):
    ny = v.shape[0]
    me, n = lax.axis_index("gy"), lax.axis_size("gy")
    row = lax.broadcasted_iota(jnp.int32, v.shape, 0)
    ahead = jnp.where(row == ny - 1, 0.0, pltpu.roll(v, ny - 1, 0))
    behind = jnp.where(row == 0, 0.0, pltpu.roll(v, 1, 0))
    east, west = lateral - half, lateral + half
    inside_high = (row == ny - 1) & (me < n - 1)
    inside_low = (row == 0) & (me > 0)
    side = jnp.where(inside_high, east, jnp.where(inside_low, west, 0.0))
    return east * (ahead - v) + west * (behind - v), side


def vertical_step(nz, v, column, lateral, half):
    upper = lax.axis_index("gz")
    lane = lax.broadcasted_iota(jnp.int32, v.shape, 1)
    column = jnp.broadcast_to(column, v.shape)
    ahead = jnp.where(lane == nz - 1, jnp.where(upper == 0, column, 0.0), pltpu.roll(v, nz - 1, 1))
    behind = jnp.where(lane == 0, jnp.where(upper == 0, 0.0, column), pltpu.roll(v, 1, 1))
    return (lateral - half) * (ahead - v) + (lateral + half) * (behind - v)


def ghost_kernel(nx, tiles, gi, gm, gu, gq, gr, own):
    ghost = Ghost(tiles.shape[1:], nx)

    def keep(ref):
        def store(k, v):
            ref[k] = v

        return store

    ports = factor(
        nx,
        lambda k: ghost.named(tiles, "lat", k),
        lambda k: 0.5 * ghost.named(tiles, "cx", k),
        ghost.ratio,
        *(keep(ref) for ref in (gi, gm, gu, gq, gr)),
    )
    for v in range(4):
        own[v] = ports[v]


def early_kernel(
    nx, nz, t, h, load, lat, up, cy, cz, mine, tiles, d, side, gd, gside
):
    upper = lax.axis_index("gz")
    ghost = Ghost(tiles.shape[1:], nx)
    for k in range(nx):
        v = ghost.fields(tiles, 0, k)
        lateral = ghost.ratio * ghost.named(tiles, "lat", k)
        step, gside[k] = lateral_step(v, lateral, 0.5 * ghost.named(tiles, "cy", k))
        inner, here = ghost.fields(tiles, 2, k), ghost.fields(mine, 0, k)
        ahead, behind = jnp.where(upper == 0, inner, here), jnp.where(upper == 0, here, inner)
        rise, half = ghost.ratio * ghost.named(tiles, "up", k), 0.5 * ghost.named(tiles, "cz", k)
        step = step + ((rise - half) * (ahead - v) + (rise + half) * (behind - v))
        gd[k] = v + step + jnp.where(ghost.first, ghost.named(tiles, "load", k), 0.0)
    for f, (ratio, ref) in enumerate(zip(RATIOS, (t, h))):
        for k in range(nx):
            v = ref[k]
            step, side[f, k] = lateral_step(v, ratio * lat[k], 0.5 * cy[k])
            at = nx * f + k
            out = v + step + vertical_step(
                nz, v, tiles[0, :, at : at + 1], ratio * up[k], 0.5 * cz[k]
            )
            d[f, k] = out + load[k] if f == 0 else out


def first_kernel(
    paired, nx, ny, faces, d0, side, gd, gside, xi, xm, xu, gi, gm, gu, own, near, gown, gnear,
    d, p, gp, ends, *word
):
    odd = lax.axis_index("gy") % 2
    half = ny // 2
    slopes = []
    for f in range(2):
        for k in range(nx):
            low = faces[1 - odd, f, pl.ds(k, half, stride=0), :]
            high = faces[odd, f, pl.ds(k, half, stride=0), :]
            d[f, k, :half] = d0[f, k, :half] + side[f, k, :half] * low
            d[f, k, half:] = d0[f, k, half:] + side[f, k, half:] * high
        mine = sweep(
            nx, lambda k: d[f, k], lambda k: xi[f, k], lambda k: xm[f, k], lambda k: xu[f, k], put(p, f)
        )
        ends[2 * f], ends[2 * f + 1] = mine
        if paired:
            word[0][f], slope = pair_source("gx", mine, coefs_of(own, f), coefs_of(near, f))
            slopes.append(slope)
    low_row = faces[1 - odd, 2, pl.ds(ny - 1, half, stride=0), :]
    high_row = faces[odd, 2, pl.ds(0, half, stride=0), :]
    first = lax.broadcasted_iota(jnp.int32, low_row.shape, 1) < low_row.shape[1] // 2

    def spread(row, k):
        a = jnp.broadcast_to(row[:, k : k + 1], row.shape)
        b = jnp.broadcast_to(row[:, nx + k : nx + k + 1], row.shape)
        return jnp.where(first, a, b)

    def rhs(k):
        beside_rows = jnp.concatenate([spread(low_row, k), spread(high_row, k)])
        return gd[k] + gside[k] * beside_rows

    def keep(k, v):
        gp[k] = v

    mine = sweep(nx, rhs, lambda k: gi[k], lambda k: gm[k], lambda k: gu[k], keep)
    ends[4] = packed(*mine)
    if paired:
        word[0][2] = packed(*pair_source("gx", mine, x_coefs(own, gown, 2), x_coefs(near, gnear, 2)))
        word[0][3] = jnp.where(place("gx")[2] == 0, slopes[0], slopes[1])


def packed(a, b):
    lane = lax.broadcasted_iota(jnp.int32, a.shape, 1)
    return jnp.where((lane & 32) == 0, a, b)


def unpacked(both):
    lane = lax.broadcasted_iota(jnp.int32, both.shape, 1)
    a = jnp.where((lane & 32) == 0, both, pltpu.roll(both, 32, 1))
    b = jnp.where((lane & 32) == 0, pltpu.roll(both, both.shape[1] - 32, 1), both)
    return a, b


def x_ends(ends, f):
    return (ends[2 * f], ends[2 * f + 1]) if f < 2 else unpacked(ends[4])


def x_coefs(own, ghost, f):
    return coefs_of(own, f) if f < 2 else tuple(ghost[v] for v in range(4))


def second_kernel(
    paired, nx, ny, nz, p, q, r, gp, gq, gr, ends, near_ends, own, near, gown, gnear,
    d, load, up, cz, yi, ym, yu, yown, ynear, *rest,
):
    far, (py, *outs, s) = rest[: 1 + paired[0]], rest[1 + paired[0] :]

    def values(f):
        mine, coefs = x_ends(ends, f), x_coefs(own, gown, f)
        if paired[0]:
            two, three = far
            if f < 2:
                word = two[f] + three[f], jnp.where(place("gx")[2] == f, two[3], three[3])
            else:
                word, more = unpacked(two[2]), unpacked(three[2])
                word = word[0] + more[0], word[1]
            other, other_coefs = x_ends(near_ends, f), x_coefs(near, gnear, f)
            return pair_values("gx", mine, other, coefs, other_coefs, word)

        def port_of(j):
            theirs = x_ends(far[0].at[j], f)
            at = [5 + 2 * v + f if f < 2 else 13 + v for v in range(4)]
            return tuple(theirs) + tuple(far[0][j, i] for i in at)

        return scan_values("gx", tuple(mine) + coefs, port_of)

    ghost_low, ghost_high = values(2)
    for f, ratio in enumerate(RATIOS):
        low, high = values(f)
        for k in range(nx):
            v = p[f, k] + q[f, k] * low + r[f, k] * high
            beyond = gp[k] + gq[k] * ghost_low + gr[k] * ghost_high
            at = f * nz // 2
            out = 2.0 * v - d[f, k]
            out = out + vertical_step(nz, v, beyond[:, at : at + 1], ratio * up[k], 0.5 * cz[k])
            if f == 0:
                out = out + load[k]
            s[f, pl.ds(k * ny, ny), :] = out
        mine = sweep(
            ny,
            lambda k: s[f, pl.ds(k, nx, stride=ny), :],
            lambda k: yi[f, k],
            lambda k: ym[f, k],
            lambda k: yu[f, k],
            put(py, f),
        )
        outs[0][2 * f], outs[0][2 * f + 1] = mine
        if paired[1]:
            outs[1][f] = pair_source("gy", mine, coefs_of(yown, f), coefs_of(ynear, f))[0]


def new_kernel(paired, nx, ny, p, q, r, ends, near_ends, own, near, slopes, *rest):
    received, news = rest[:-2], rest[-2:]
    for f, ref in enumerate(news):
        mine = (ends[2 * f], ends[2 * f + 1])
        coefs = coefs_of(own, f)
        if paired:
            other = (near_ends[2 * f], near_ends[2 * f + 1])
            two, three = received
            low, high = pair_values(
                "gy", mine, other, coefs, coefs_of(near, f), (two[f] + three[f], slopes[f])
            )
        else:
            (ports,) = received

            def port_of(j):
                return (ports[j, 2 * f], ports[j, 2 * f + 1]) + tuple(
                    ports[j, 4 + 2 * v + f] for v in range(4)
                )

            low, high = scan_values("gy", mine + coefs, port_of)
        for k in range(ny):
            ref[pl.ds(k, nx, stride=ny), :] = p[f, k] + q[f, k] * low + r[f, k] * high


def neighbours(one, two):
    across, n = lax.axis_size("gx"), lax.axis_size("gy")

    def swapped(first, value):
        partner = {i: i ^ 1 if first == 0 else ((i + 1) ^ 1) - 1 for i in range(n)}
        pairs = []
        for x in range(across):
            for i in range(n):
                j = partner[i]
                target = (x, j) if 0 <= j < n else (x ^ 1, i)
                if target[0] < across:
                    pairs.append((x * n + i, target[0] * n + target[1]))
        return lax.ppermute(value, ("gx", "gy"), pairs)

    return swapped(0, one), swapped(1, two)


def body(thermal, vapour, load, lat, up, cx, cy, cz):
    nx, ny, nz = thermal.shape
    assert lax.axis_size("gz") == 2 and nx * 8 == nz
    flat = (nx * ny, nz)
    lines_x, lines_y = (2, nx, ny, nz), (2, ny, nx, nz)
    block_x, block_y = (ny, nz), (nx, nz)
    paired = (lax.axis_size("gx") == 4, lax.axis_size("gy") == 4)
    thermal, vapour, load, lat, up, cx, cy, cz, mine = call(
        functools.partial(open_kernel, nx, nz),
        (thermal.shape,) * 8 + ((2,) + block_x,),
        *(
            pltpu.with_memory_space_constraint(a, pltpu.HBM)
            for a in (thermal, vapour, load, lat, up, cx, cy, cz)
        ),
        scratch=[pltpu.SemaphoreType.DMA((8,))],
        space=pltpu.HBM,
    )
    tiles = swap(mine, "gz", 1)
    xi, xm, xu, xq, xr, yi, ym, yu, yq, yr, xown, yown, one, two = call(
        functools.partial(coef_kernel, nx, ny),
        (lines_x,) * 5
        + (lines_y,) * 5
        + ((4, 2) + block_x, (4, 2) + block_y, (2,) + block_y, (2,) + block_y),
        *(a.reshape(flat) for a in (thermal, vapour, lat, cx, cy)),
    )
    xnear, ynear, yslopes = xown, yown, yown[0]
    if paired[0]:
        xnear = swap(xown, "gx", 1)
    if paired[1]:
        ynear = swap(yown, "gy", 1)
        (yslopes,) = call(functools.partial(slope_kernel, "gy"), ((2,) + block_y,), yown, ynear)
        yslopes = swap(yslopes, "gy", 3)
    one, two = neighbours(
        jnp.concatenate([one, tiles[:1]]), jnp.concatenate([two, tiles[:1]])
    )
    gi, gm, gu, gq, gr, gown = call(
        functools.partial(ghost_kernel, nx), ((nx,) + block_x,) * 5 + ((4,) + block_x,), tiles
    )
    d, side, gd, gside = call(
        functools.partial(early_kernel, nx, nz),
        (lines_x, lines_x) + ((nx,) + block_x,) * 2,
        thermal, vapour, load, lat, up, cy, cz, mine, tiles,
    )
    gnear = swap(gown, "gx", 1) if paired[0] else gown
    d, p, gp, ends, *word = call(
        functools.partial(first_kernel, paired[0], nx, ny),
        (lines_x, lines_x, (nx,) + block_x, (5,) + block_x) + ((4,) + block_x,) * paired[0],
        jnp.stack([one, two]), d, side, gd, gside, xi, xm, xu, gi, gm, gu, xown, xnear, gown, gnear,
    )
    if paired[0]:
        near_ends = swap(ends, "gx", 1)
        far = [swap(word[0], "gx", k) for k in (2, 3)]
    else:
        near_ends, far = ends, [everyones("gx", ends, xown, gown)]
    py, yends, *outs = call(
        functools.partial(second_kernel, paired, nx, ny, nz),
        (lines_y, (4,) + block_y) + (((2,) + block_y,) if paired[1] else ()),
        p, xq, xr, gp, gq, gr, ends, near_ends, xown, xnear, gown, gnear,
        d, load, up, cz, yi, ym, yu, yown, ynear, *far,
        scratch=[pltpu.VMEM((2,) + flat, F32)],
    )
    if paired[1]:
        received = [swap(outs[0], "gy", k) for k in (2, 3)]
        near_ends = swap(yends, "gy", 1)
    else:
        near_ends, received = yends, [everyones("gy", yends, yown)]
    t_new, h_new = call(
        functools.partial(new_kernel, paired[1], nx, ny),
        (flat, flat),
        py, yq, yr, yends, near_ends, yown, ynear, yslopes, *received,
    )
    return t_new.reshape(thermal.shape), h_new.reshape(thermal.shape)


def solution(mesh):
    spec = P("gx", "gy", "gz")
    return jax.shard_map(
        body, mesh=mesh, in_specs=(spec,) * 8, out_specs=(spec, spec), check_vma=False
    )
```

```python
import functools

import jax
import jax.numpy as jnp
from jax import lax
from jax.experimental import pallas as pl
from jax.experimental.pallas import tpu as pltpu
from jax.sharding import PartitionSpec as P


RATIOS = (1.0, 0.8)
F32 = jnp.float32


def vmem():
    return pl.BlockSpec(memory_space=pltpu.VMEM)


def call(kernel, outs, *args, scratch=(), flops=400000, space=pltpu.VMEM):
    size = sum(4 * a.size for a in args)
    return run(kernel, outs, args, scratch, flops, size, space)


def run(kernel, outs, args, scratch, flops, size, space):
    return pl.pallas_call(
        kernel,
        out_shape=tuple(jax.ShapeDtypeStruct(s, F32) for s in outs),
        in_specs=[pl.BlockSpec(memory_space=space)] * len(args),
        out_specs=tuple(vmem() for _ in outs),
        scratch_shapes=list(scratch),
        compiler_params=pltpu.CompilerParams(vmem_limit_bytes=8 << 20),
        cost_estimate=pl.CostEstimate(flops=flops, bytes_accessed=size, transcendentals=0),
    )(*args)


def factor(n, lat, half_cfl, ratio, inv_out, mid_out, up_out, first_out, last_out):
    ups, firsts = [], []
    up = first = None
    for k in range(n):
        lateral = ratio * lat(k)
        half = half_cfl(k)
        east, west = lateral - half, lateral + half
        pivot = 1.0 + 2.0 * lateral
        if k:
            pivot = pivot - west * up
        inverse = 1.0 / pivot
        mid = west * inverse
        up = east * inverse
        first = mid if k == 0 else mid * first
        inv_out(k, inverse)
        mid_out(k, mid)
        up_out(k, up)
        ups.append(up)
        firsts.append(first)
    q, r = firsts[-1], ups[-1]
    first_out(n - 1, q)
    last_out(n - 1, r)
    q2, r2 = q, r
    for k in range(n - 2, -1, -1):
        q = firsts[k] + ups[k] * q
        r = ups[k] * r
        first_out(k, q)
        last_out(k, r)
    return q, q2, r, r2


def sweep(n, rhs, inv, mid, up, out):
    values = []
    value = None
    for k in range(n):
        value = inv(k) * rhs(k) if k == 0 else inv(k) * rhs(k) + mid(k) * value
        values.append(value)
    out(n - 1, value)
    last = value
    for k in range(n - 2, -1, -1):
        value = values[k] + up(k) * value
        out(k, value)
    return value, last


def along(port, before):
    p1, p2, q1, q2, r1, r2 = port
    source, slope = before
    t = 1.0 / (1.0 - q1 * slope)
    step = q2 * slope * t
    return p2 + q2 * source + step * (p1 + q1 * source), r2 + step * r1


def mirrored(port):
    p1, p2, q1, q2, r1, r2 = port
    return p2, p1, r2, r1, q2, q1


def pick(flag, a, b):
    return tuple(jnp.where(flag, x, y) for x, y in zip(a, b))


def beside(port, left, right):
    p1, p2, q1, q2, r1, r2 = port
    pl_, ql = left
    pr, qr = right
    a1 = p1 + q1 * pl_ + r1 * pr
    a2 = p2 + q2 * pl_ + r2 * pr
    b11, b22 = 1.0 - q1 * ql, 1.0 - r2 * qr
    b12, b21 = r1 * qr, q2 * ql
    t = 1.0 / (b11 * b22 - b12 * b21)
    u1 = (a1 * b22 + b12 * a2) * t
    u2 = (b11 * a2 + b21 * a1) * t
    return pl_ + ql * u1, pr + qr * u2


def place(axis):
    me = lax.axis_index(axis)
    second = me // 2
    return second == 1, second == me % 2, me % 2


def coefs_of(ref, f):
    return tuple(ref[v, f] for v in range(4))


def oriented(axis, ends, coefs):
    port = tuple(ends) + tuple(coefs)
    return pick(place(axis)[0], mirrored(port), port)


def pair_source(axis, ends, own, near):
    outer = place(axis)[1]
    zero = jnp.zeros_like(own[0])
    mine = oriented(axis, ends or (zero, zero), own)
    other = oriented(axis, (zero, zero), near)
    q1, q2, r1, r2 = pick(outer, other[2:], mine[2:])
    slope = jnp.where(outer, mine[5], other[5])
    step = q2 / (1.0 - q1 * slope)
    part = jnp.where(outer, step * mine[1], mine[1] + step * slope * mine[0])
    return part, r2 + step * slope * r1


def pair_values(axis, ends, near_ends, own, near, far):
    second, outer, _ = place(axis)
    zero = jnp.zeros_like(ends[0])
    mine = oriented(axis, ends, own)
    other = oriented(axis, near_ends, near)
    ahead = pick(outer, along(mirrored(other), far), far)
    behind = pick(outer, (zero, zero), (other[1], other[5]))
    back, front = beside(mine, behind, ahead)
    return pick(second, (front, back), (back, front))


def near_word(axis, ends, own, slope):
    mine = oriented(axis, ends, own)
    r1, r2 = mine[4:]
    inner = mine[0] + r1 * slope / (1.0 - r2 * slope) * mine[1]
    return jnp.where(place(axis)[1], mine[1], inner)


def word_values(axis, ends, word, own, near, far):
    second, outer, _ = place(axis)
    zero = jnp.zeros_like(word)
    source, slope = far
    mine = oriented(axis, ends, own)
    q1, q2, r1, r2 = oriented(axis, (zero, zero), near)[2:]
    step = r1 * slope / (1.0 - r2 * slope)
    ahead = pick(outer, (word + (r1 + step * r2) * source, q1 + step * q2), far)
    behind = pick(outer, (zero, zero), (word, r2))
    back, front = beside(mine, behind, ahead)
    return pick(second, (front, back), (back, front))


def scan_values(axis, mine, port_of):
    me, n = lax.axis_index(axis), lax.axis_size(axis)
    zero = jnp.zeros_like(mine[0])

    def step(j, sides):
        left, right = sides
        left = pick(j < me, along(port_of(j), left), left)
        i = n - 1 - j
        right = pick(i > me, along(mirrored(port_of(i)), right), right)
        return left, right

    left, right = lax.fori_loop(0, n, step, ((zero, zero), (zero, zero)))
    return beside(mine, left, right)


def everyones(axis, ends, own, *more):
    return lax.all_gather(
        jnp.concatenate([ends, own.reshape((8,) + own.shape[2:]), *more]), axis
    )


def swap(value, axis, k):
    return lax.ppermute(value, axis, [(i, i ^ k) for i in range(lax.axis_size(axis))])


PLANES = ("load", "lat", "up", "cx", "cy", "cz")


def open_kernel(nx, nz, *refs):
    ins, outs, tiles, sems = refs[:8], refs[8:16], refs[16], refs[17]
    copies = [pltpu.make_async_copy(a, b, sems.at[i]) for i, (a, b) in enumerate(zip(ins, outs))]
    for copy in copies:
        copy.start()
    upper = lax.axis_index("gz")
    edge, inner = 1 - upper, 2 - 3 * upper
    planes = [(0, edge), (1, edge), (0, inner), (1, inner)] + [(i, edge) for i in range(2, 8)]
    lane = lax.broadcasted_iota(jnp.int32, outs[0].shape[1:], 1)

    def plane(a, i, offset):
        moved = [
            pltpu.roll(outs[i][k], lax.rem(offset + (nx * a + k + nz), nz), 1) for k in range(nx)
        ]
        bit = 1
        while len(moved) > 1:
            moved = [jnp.where((lane & bit) == 0, x, y) for x, y in zip(moved[::2], moved[1::2])]
            bit *= 2
        return moved[0]

    per_tile = nz // nx
    packed = []
    for group in (range(2), range(2, 8)):
        for i in group:
            copies[i].wait()
        for n, (i, offset) in enumerate(planes):
            if i in group:
                packed.append((n, plane(n % per_tile, i, offset)))
    for first in range(0, len(planes), per_tile):
        tile = None
        for n, part in packed:
            if first <= n < first + per_tile:
                at = nx * (n - first)
                tile = part if tile is None else jnp.where(lane < at, tile, part)
        tiles[first // per_tile] = tile


def put(ref, f):
    def store(k, v):
        ref[f, k] = v

    return store


def coef_kernel(nx, ny, t, h, lat, cx, cy, xi, xm, xu, xq, xr, yi, ym, yu, yq, yr, xown, yown, one, two):
    even = lax.axis_index("gy") % 2 == 0
    for f, (ratio, ref) in enumerate(zip(RATIOS, (t, h))):
        low = ref[pl.ds(0, nx, stride=ny), :]
        high = ref[pl.ds(ny - 1, nx, stride=ny), :]
        one[f] = jnp.where(even, high, low)
        two[f] = jnp.where(even, low, high)
    for f, ratio in enumerate(RATIOS):
        own = factor(
            nx,
            lambda k: lat[pl.ds(k * ny, ny), :],
            lambda k: 0.5 * cx[pl.ds(k * ny, ny), :],
            ratio,
            *(put(ref, f) for ref in (xi, xm, xu, xq, xr)),
        )
        for v in range(4):
            xown[v, f] = own[v]
        own = factor(
            ny,
            lambda k: lat[pl.ds(k, nx, stride=ny), :],
            lambda k: 0.5 * cy[pl.ds(k, nx, stride=ny), :],
            ratio,
            *(put(ref, f) for ref in (yi, ym, yu, yq, yr)),
        )
        for v in range(4):
            yown[v, f] = own[v]


def slope_kernel(axis, own, near, out):
    for f in range(2):
        out[f] = pair_source(axis, None, coefs_of(own, f), coefs_of(near, f))[1]


class Ghost:
    def __init__(self, shape, nx):
        self.shape, self.nx = shape, nx
        self.first = lax.broadcasted_iota(jnp.int32, shape, 1) < shape[1] // 2
        self.ratio = jnp.where(self.first, RATIOS[0], RATIOS[1])

    def lane(self, tiles, plane, k):
        at = self.nx * plane + k
        column = tiles[at // self.shape[1], :, at % self.shape[1] : at % self.shape[1] + 1]
        return jnp.broadcast_to(column, self.shape)

    def fields(self, tiles, plane, k):
        return jnp.where(self.first, self.lane(tiles, plane, k), self.lane(tiles, plane + 1, k))

    def named(self, tiles, name, k):
        return self.lane(tiles, 4 + PLANES.index(name), k)


def lateral_step(v, lateral, half):
    ny = v.shape[0]
    me, n = lax.axis_index("gy"), lax.axis_size("gy")
    row = lax.broadcasted_iota(jnp.int32, v.shape, 0)
    ahead = jnp.where(row == ny - 1, 0.0, pltpu.roll(v, ny - 1, 0))
    behind = jnp.where(row == 0, 0.0, pltpu.roll(v, 1, 0))
    east, west = lateral - half, lateral + half
    inside_high = (row == ny - 1) & (me < n - 1)
    inside_low = (row == 0) & (me > 0)
    side = jnp.where(inside_high, east, jnp.where(inside_low, west, 0.0))
    return east * (ahead - v) + west * (behind - v), side


def vertical_step(nz, v, column, lateral, half):
    upper = lax.axis_index("gz")
    lane = lax.broadcasted_iota(jnp.int32, v.shape, 1)
    column = jnp.broadcast_to(column, v.shape)
    ahead = jnp.where(lane == nz - 1, jnp.where(upper == 0, column, 0.0), pltpu.roll(v, nz - 1, 1))
    behind = jnp.where(lane == 0, jnp.where(upper == 0, 0.0, column), pltpu.roll(v, 1, 1))
    return (lateral - half) * (ahead - v) + (lateral + half) * (behind - v)


def ghost_kernel(nx, tiles, gi, gm, gu, gq, gr, own):
    ghost = Ghost(tiles.shape[1:], nx)

    def keep(ref):
        def store(k, v):
            ref[k] = v

        return store

    ports = factor(
        nx,
        lambda k: ghost.named(tiles, "lat", k),
        lambda k: 0.5 * ghost.named(tiles, "cx", k),
        ghost.ratio,
        *(keep(ref) for ref in (gi, gm, gu, gq, gr)),
    )
    for v in range(4):
        own[v] = ports[v]


def early_kernel(
    nx, nz, t, h, load, lat, up, cy, cz, mine, tiles, d, side, gd, gside
):
    upper = lax.axis_index("gz")
    ghost = Ghost(tiles.shape[1:], nx)
    for k in range(nx):
        v = ghost.fields(tiles, 0, k)
        lateral = ghost.ratio * ghost.named(tiles, "lat", k)
        step, gside[k] = lateral_step(v, lateral, 0.5 * ghost.named(tiles, "cy", k))
        inner, here = ghost.fields(tiles, 2, k), ghost.fields(mine, 0, k)
        ahead, behind = jnp.where(upper == 0, inner, here), jnp.where(upper == 0, here, inner)
        rise, half = ghost.ratio * ghost.named(tiles, "up", k), 0.5 * ghost.named(tiles, "cz", k)
        step = step + ((rise - half) * (ahead - v) + (rise + half) * (behind - v))
        gd[k] = v + step + jnp.where(ghost.first, ghost.named(tiles, "load", k), 0.0)
    for f, (ratio, ref) in enumerate(zip(RATIOS, (t, h))):
        for k in range(nx):
            v = ref[k]
            step, side[f, k] = lateral_step(v, ratio * lat[k], 0.5 * cy[k])
            at = nx * f + k
            out = v + step + vertical_step(
                nz, v, tiles[0, :, at : at + 1], ratio * up[k], 0.5 * cz[k]
            )
            d[f, k] = out + load[k] if f == 0 else out


def first_kernel(
    paired, nx, ny, faces, d0, side, gd, gside, xi, xm, xu, gi, gm, gu, own, near, gown, gnear,
    d, p, gp, ends, *word
):
    odd = lax.axis_index("gy") % 2
    half = ny // 2
    slopes = []
    for f in range(2):
        for k in range(nx):
            low = faces[1 - odd, f, pl.ds(k, half, stride=0), :]
            high = faces[odd, f, pl.ds(k, half, stride=0), :]
            d[f, k, :half] = d0[f, k, :half] + side[f, k, :half] * low
            d[f, k, half:] = d0[f, k, half:] + side[f, k, half:] * high
        mine = sweep(
            nx, lambda k: d[f, k], lambda k: xi[f, k], lambda k: xm[f, k], lambda k: xu[f, k], put(p, f)
        )
        ends[2 * f], ends[2 * f + 1] = mine
        if paired:
            word[0][f], slope = pair_source("gx", mine, coefs_of(own, f), coefs_of(near, f))
            slopes.append(slope)
    low_row = faces[1 - odd, 2, pl.ds(ny - 1, half, stride=0), :]
    high_row = faces[odd, 2, pl.ds(0, half, stride=0), :]
    first = lax.broadcasted_iota(jnp.int32, low_row.shape, 1) < low_row.shape[1] // 2

    def spread(row, k):
        a = jnp.broadcast_to(row[:, k : k + 1], row.shape)
        b = jnp.broadcast_to(row[:, nx + k : nx + k + 1], row.shape)
        return jnp.where(first, a, b)

    def rhs(k):
        beside_rows = jnp.concatenate([spread(low_row, k), spread(high_row, k)])
        return gd[k] + gside[k] * beside_rows

    def keep(k, v):
        gp[k] = v

    mine = sweep(nx, rhs, lambda k: gi[k], lambda k: gm[k], lambda k: gu[k], keep)
    ends[4] = packed(*mine)
    if paired:
        word[0][2] = packed(*pair_source("gx", mine, x_coefs(own, gown, 2), x_coefs(near, gnear, 2)))
        word[0][3] = jnp.where(place("gx")[2] == 0, slopes[0], slopes[1])


def packed(a, b):
    lane = lax.broadcasted_iota(jnp.int32, a.shape, 1)
    return jnp.where((lane & 32) == 0, a, b)


def unpacked(both):
    lane = lax.broadcasted_iota(jnp.int32, both.shape, 1)
    a = jnp.where((lane & 32) == 0, both, pltpu.roll(both, 32, 1))
    b = jnp.where((lane & 32) == 0, pltpu.roll(both, both.shape[1] - 32, 1), both)
    return a, b


def x_ends(ends, f):
    return (ends[2 * f], ends[2 * f + 1]) if f < 2 else unpacked(ends[4])


def x_coefs(own, ghost, f):
    return coefs_of(own, f) if f < 2 else tuple(ghost[v] for v in range(4))


def second_kernel(
    paired, nx, ny, nz, p, q, r, gp, gq, gr, ends, near_ends, own, near, gown, gnear,
    d, load, up, cz, yi, ym, yu, yown, ynear, *rest,
):
    far, (py, *outs, s) = rest[: 1 + paired[0]], rest[1 + paired[0] :]

    def values(f):
        mine, coefs = x_ends(ends, f), x_coefs(own, gown, f)
        if paired[0]:
            two, three = far
            if f < 2:
                word = two[f] + three[f], jnp.where(place("gx")[2] == f, two[3], three[3])
            else:
                word, more = unpacked(two[2]), unpacked(three[2])
                word = word[0] + more[0], word[1]
            other, other_coefs = x_ends(near_ends, f), x_coefs(near, gnear, f)
            return pair_values("gx", mine, other, coefs, other_coefs, word)

        def port_of(j):
            theirs = x_ends(far[0].at[j], f)
            at = [5 + 2 * v + f if f < 2 else 13 + v for v in range(4)]
            return tuple(theirs) + tuple(far[0][j, i] for i in at)

        return scan_values("gx", tuple(mine) + coefs, port_of)

    ghost_low, ghost_high = values(2)
    for f, ratio in enumerate(RATIOS):
        low, high = values(f)
        for k in range(nx):
            v = p[f, k] + q[f, k] * low + r[f, k] * high
            beyond = gp[k] + gq[k] * ghost_low + gr[k] * ghost_high
            at = f * nz // 2
            out = 2.0 * v - d[f, k]
            out = out + vertical_step(nz, v, beyond[:, at : at + 1], ratio * up[k], 0.5 * cz[k])
            if f == 0:
                out = out + load[k]
            s[f, pl.ds(k * ny, ny), :] = out
        mine = sweep(
            ny,
            lambda k: s[f, pl.ds(k, nx, stride=ny), :],
            lambda k: yi[f, k],
            lambda k: ym[f, k],
            lambda k: yu[f, k],
            put(py, f),
        )
        outs[0][2 * f], outs[0][2 * f + 1] = mine
        if paired[1]:
            outs[1][f] = pair_source("gy", mine, coefs_of(yown, f), coefs_of(ynear, f))[0]


def word_kernel(ends, own, slopes, out):
    for f in range(2):
        out[f] = near_word("gy", (ends[2 * f], ends[2 * f + 1]), coefs_of(own, f), slopes[f])


def new_kernel(paired, nx, ny, p, q, r, ends, word, own, near, slopes, *rest):
    received, news = rest[:-2], rest[-2:]
    for f, ref in enumerate(news):
        mine = (ends[2 * f], ends[2 * f + 1])
        coefs = coefs_of(own, f)
        if paired:
            two, three = received
            far = two[f] + three[f], slopes[f]
            low, high = word_values("gy", mine, word[f], coefs, coefs_of(near, f), far)
        else:
            (ports,) = received

            def port_of(j):
                return (ports[j, 2 * f], ports[j, 2 * f + 1]) + tuple(
                    ports[j, 4 + 2 * v + f] for v in range(4)
                )

            low, high = scan_values("gy", mine + coefs, port_of)
        for k in range(ny):
            ref[pl.ds(k, nx, stride=ny), :] = p[f, k] + q[f, k] * low + r[f, k] * high


def neighbours(one, two):
    across, n = lax.axis_size("gx"), lax.axis_size("gy")

    def swapped(first, value):
        partner = {i: i ^ 1 if first == 0 else ((i + 1) ^ 1) - 1 for i in range(n)}
        pairs = []
        for x in range(across):
            for i in range(n):
                j = partner[i]
                target = (x, j) if 0 <= j < n else (x ^ 1, i)
                if target[0] < across:
                    pairs.append((x * n + i, target[0] * n + target[1]))
        return lax.ppermute(value, ("gx", "gy"), pairs)

    return swapped(0, one), swapped(1, two)


def body(thermal, vapour, load, lat, up, cx, cy, cz):
    nx, ny, nz = thermal.shape
    assert lax.axis_size("gz") == 2 and nx * 8 == nz
    flat = (nx * ny, nz)
    lines_x, lines_y = (2, nx, ny, nz), (2, ny, nx, nz)
    block_x, block_y = (ny, nz), (nx, nz)
    paired = (lax.axis_size("gx") == 4, lax.axis_size("gy") == 4)
    thermal, vapour, load, lat, up, cx, cy, cz, mine = call(
        functools.partial(open_kernel, nx, nz),
        (thermal.shape,) * 8 + ((2,) + block_x,),
        *(
            pltpu.with_memory_space_constraint(a, pltpu.HBM)
            for a in (thermal, vapour, load, lat, up, cx, cy, cz)
        ),
        scratch=[pltpu.SemaphoreType.DMA((8,))],
        space=pltpu.HBM,
    )
    tiles = swap(mine, "gz", 1)
    xi, xm, xu, xq, xr, yi, ym, yu, yq, yr, xown, yown, one, two = call(
        functools.partial(coef_kernel, nx, ny),
        (lines_x,) * 5
        + (lines_y,) * 5
        + ((4, 2) + block_x, (4, 2) + block_y, (2,) + block_y, (2,) + block_y),
        *(a.reshape(flat) for a in (thermal, vapour, lat, cx, cy)),
    )
    xnear, ynear, yslopes = xown, yown, yown[0]
    if paired[0]:
        xnear = swap(xown, "gx", 1)
    if paired[1]:
        ynear = swap(yown, "gy", 1)
        (yslopes,) = call(functools.partial(slope_kernel, "gy"), ((2,) + block_y,), yown, ynear)
        yslopes = swap(yslopes, "gy", 3)
    one, two = neighbours(
        jnp.concatenate([one, tiles[:1]]), jnp.concatenate([two, tiles[:1]])
    )
    gi, gm, gu, gq, gr, gown = call(
        functools.partial(ghost_kernel, nx), ((nx,) + block_x,) * 5 + ((4,) + block_x,), tiles
    )
    d, side, gd, gside = call(
        functools.partial(early_kernel, nx, nz),
        (lines_x, lines_x) + ((nx,) + block_x,) * 2,
        thermal, vapour, load, lat, up, cy, cz, mine, tiles,
    )
    gnear = swap(gown, "gx", 1) if paired[0] else gown
    d, p, gp, ends, *word = call(
        functools.partial(first_kernel, paired[0], nx, ny),
        (lines_x, lines_x, (nx,) + block_x, (5,) + block_x) + ((4,) + block_x,) * paired[0],
        jnp.stack([one, two]), d, side, gd, gside, xi, xm, xu, gi, gm, gu, xown, xnear, gown, gnear,
    )
    if paired[0]:
        near_ends = swap(ends, "gx", 1)
        far = [swap(word[0], "gx", k) for k in (2, 3)]
    else:
        near_ends, far = ends, [everyones("gx", ends, xown, gown)]
    py, yends, *outs = call(
        functools.partial(second_kernel, paired, nx, ny, nz),
        (lines_y, (4,) + block_y) + (((2,) + block_y,) if paired[1] else ()),
        p, xq, xr, gp, gq, gr, ends, near_ends, xown, xnear, gown, gnear,
        d, load, up, cz, yi, ym, yu, yown, ynear, *far,
        scratch=[pltpu.VMEM((2,) + flat, F32)],
    )
    if paired[1]:
        received = [swap(outs[0], "gy", k) for k in (2, 3)]
        (word,) = call(word_kernel, ((2,) + block_y,), yends, yown, yslopes)
        word = swap(word, "gy", 1)
    else:
        word, received = yends, [everyones("gy", yends, yown)]
    t_new, h_new = call(
        functools.partial(new_kernel, paired[1], nx, ny),
        (flat, flat),
        py, yq, yr, yends, word, yown, ynear, yslopes, *received,
    )
    return t_new.reshape(thermal.shape), h_new.reshape(thermal.shape)


def solution(mesh):
    spec = P("gx", "gy", "gz")
    return jax.shard_map(
        body, mesh=mesh, in_specs=(spec,) * 8, out_specs=(spec, spec), check_vma=False
    )
```

```python
import functools

import jax
import jax.numpy as jnp
from jax import lax
from jax.experimental import pallas as pl
from jax.experimental.pallas import tpu as pltpu
from jax.sharding import PartitionSpec as P


RATIOS = (1.0, 0.8)
F32 = jnp.float32


def vmem():
    return pl.BlockSpec(memory_space=pltpu.VMEM)


def call(kernel, outs, *args, scratch=(), flops=400000, space=pltpu.VMEM):
    size = sum(4 * a.size for a in args)
    return run(kernel, outs, args, scratch, flops, size, space)


def run(kernel, outs, args, scratch, flops, size, space):
    return pl.pallas_call(
        kernel,
        out_shape=tuple(jax.ShapeDtypeStruct(s, F32) for s in outs),
        in_specs=[pl.BlockSpec(memory_space=space)] * len(args),
        out_specs=tuple(vmem() for _ in outs),
        scratch_shapes=list(scratch),
        compiler_params=pltpu.CompilerParams(vmem_limit_bytes=8 << 20),
        cost_estimate=pl.CostEstimate(flops=flops, bytes_accessed=size, transcendentals=0),
    )(*args)


def factor(n, lat, half_cfl, ratio, inv_out, mid_out, up_out, first_out, last_out):
    ups, firsts = [], []
    up = first = None
    for k in range(n):
        lateral = ratio * lat(k)
        half = half_cfl(k)
        east, west = lateral - half, lateral + half
        pivot = 1.0 + 2.0 * lateral
        if k:
            pivot = pivot - west * up
        inverse = 1.0 / pivot
        mid = west * inverse
        up = east * inverse
        first = mid if k == 0 else mid * first
        inv_out(k, inverse)
        mid_out(k, mid)
        up_out(k, up)
        ups.append(up)
        firsts.append(first)
    q, r = firsts[-1], ups[-1]
    first_out(n - 1, q)
    last_out(n - 1, r)
    q2, r2 = q, r
    for k in range(n - 2, -1, -1):
        q = firsts[k] + ups[k] * q
        r = ups[k] * r
        first_out(k, q)
        last_out(k, r)
    return q, q2, r, r2


def sweep(n, rhs, inv, mid, up, out):
    values = []
    value = None
    for k in range(n):
        value = inv(k) * rhs(k) if k == 0 else inv(k) * rhs(k) + mid(k) * value
        values.append(value)
    out(n - 1, value)
    last = value
    for k in range(n - 2, -1, -1):
        value = values[k] + up(k) * value
        out(k, value)
    return value, last


def along(port, before):
    p1, p2, q1, q2, r1, r2 = port
    source, slope = before
    t = 1.0 / (1.0 - q1 * slope)
    step = q2 * slope * t
    return p2 + q2 * source + step * (p1 + q1 * source), r2 + step * r1


def mirrored(port):
    p1, p2, q1, q2, r1, r2 = port
    return p2, p1, r2, r1, q2, q1


def pick(flag, a, b):
    return tuple(jnp.where(flag, x, y) for x, y in zip(a, b))


def beside(port, left, right):
    p1, p2, q1, q2, r1, r2 = port
    pl_, ql = left
    pr, qr = right
    a1 = p1 + q1 * pl_ + r1 * pr
    a2 = p2 + q2 * pl_ + r2 * pr
    b11, b22 = 1.0 - q1 * ql, 1.0 - r2 * qr
    b12, b21 = r1 * qr, q2 * ql
    t = 1.0 / (b11 * b22 - b12 * b21)
    u1 = (a1 * b22 + b12 * a2) * t
    u2 = (b11 * a2 + b21 * a1) * t
    return pl_ + ql * u1, pr + qr * u2


def place(axis):
    me = lax.axis_index(axis)
    second = me // 2
    return second == 1, second == me % 2, me % 2


def coefs_of(ref, f):
    return tuple(ref[v, f] for v in range(4))


def oriented(axis, ends, coefs):
    port = tuple(ends) + tuple(coefs)
    return pick(place(axis)[0], mirrored(port), port)


def pair_source(axis, ends, own, near):
    outer = place(axis)[1]
    zero = jnp.zeros_like(own[0])
    mine = oriented(axis, ends or (zero, zero), own)
    other = oriented(axis, (zero, zero), near)
    q1, q2, r1, r2 = pick(outer, other[2:], mine[2:])
    slope = jnp.where(outer, mine[5], other[5])
    step = q2 / (1.0 - q1 * slope)
    part = jnp.where(outer, step * mine[1], mine[1] + step * slope * mine[0])
    return part, r2 + step * slope * r1


def pair_values(axis, ends, near_ends, own, near, far):
    second, outer, _ = place(axis)
    zero = jnp.zeros_like(ends[0])
    mine = oriented(axis, ends, own)
    other = oriented(axis, near_ends, near)
    ahead = pick(outer, along(mirrored(other), far), far)
    behind = pick(outer, (zero, zero), (other[1], other[5]))
    back, front = beside(mine, behind, ahead)
    return pick(second, (front, back), (back, front))


def near_word(axis, ends, own, slope):
    mine = oriented(axis, ends, own)
    r1, r2 = mine[4:]
    inner = mine[0] + r1 * slope / (1.0 - r2 * slope) * mine[1]
    return jnp.where(place(axis)[1], mine[1], inner)


def word_values(axis, ends, word, own, near, far):
    second, outer, _ = place(axis)
    zero = jnp.zeros_like(word)
    source, slope = far
    mine = oriented(axis, ends, own)
    q1, q2, r1, r2 = oriented(axis, (zero, zero), near)[2:]
    step = r1 * slope / (1.0 - r2 * slope)
    ahead = pick(outer, (word + (r1 + step * r2) * source, q1 + step * q2), far)
    behind = pick(outer, (zero, zero), (word, r2))
    back, front = beside(mine, behind, ahead)
    return pick(second, (front, back), (back, front))


def scan_values(axis, mine, port_of):
    me, n = lax.axis_index(axis), lax.axis_size(axis)
    zero = jnp.zeros_like(mine[0])

    def step(j, sides):
        left, right = sides
        left = pick(j < me, along(port_of(j), left), left)
        i = n - 1 - j
        right = pick(i > me, along(mirrored(port_of(i)), right), right)
        return left, right

    left, right = lax.fori_loop(0, n, step, ((zero, zero), (zero, zero)))
    return beside(mine, left, right)


def everyones(axis, ends, own, *more):
    return lax.all_gather(
        jnp.concatenate([ends, own.reshape((8,) + own.shape[2:]), *more]), axis
    )


def swap(value, axis, k):
    return lax.ppermute(value, axis, [(i, i ^ k) for i in range(lax.axis_size(axis))])


PLANES = ("load", "lat", "up", "cx", "cy", "cz")


def open_kernel(nx, nz, *refs):
    ins, outs, tiles, sems = refs[:8], refs[8:16], refs[16], refs[17]
    copies = [pltpu.make_async_copy(a, b, sems.at[i]) for i, (a, b) in enumerate(zip(ins, outs))]
    for copy in copies:
        copy.start()
    upper = lax.axis_index("gz")
    edge, inner = 1 - upper, 2 - 3 * upper
    planes = [(0, edge), (1, edge), (0, inner), (1, inner)] + [(i, edge) for i in range(2, 8)]
    lane = lax.broadcasted_iota(jnp.int32, outs[0].shape[1:], 1)

    def plane(a, i, offset):
        moved = [
            pltpu.roll(outs[i][k], lax.rem(offset + (nx * a + k + nz), nz), 1) for k in range(nx)
        ]
        bit = 1
        while len(moved) > 1:
            moved = [jnp.where((lane & bit) == 0, x, y) for x, y in zip(moved[::2], moved[1::2])]
            bit *= 2
        return moved[0]

    per_tile = nz // nx
    packed = []
    for group in (range(2), range(2, 8)):
        for i in group:
            copies[i].wait()
        for n, (i, offset) in enumerate(planes):
            if i in group:
                packed.append((n, plane(n % per_tile, i, offset)))
    for first in range(0, len(planes), per_tile):
        tile = None
        for n, part in packed:
            if first <= n < first + per_tile:
                at = nx * (n - first)
                tile = part if tile is None else jnp.where(lane < at, tile, part)
        tiles[first // per_tile] = tile


def put(ref, f):
    def store(k, v):
        ref[f, k] = v

    return store


def coef_kernel(nx, ny, t, h, lat, cx, cy, xi, xm, xu, xq, xr, yi, ym, yu, yq, yr, xown, yown, one, two):
    even = lax.axis_index("gy") % 2 == 0
    for f, (ratio, ref) in enumerate(zip(RATIOS, (t, h))):
        low = ref[pl.ds(0, nx, stride=ny), :]
        high = ref[pl.ds(ny - 1, nx, stride=ny), :]
        one[f] = jnp.where(even, high, low)
        two[f] = jnp.where(even, low, high)
    for f, ratio in enumerate(RATIOS):
        own = factor(
            nx,
            lambda k: lat[pl.ds(k * ny, ny), :],
            lambda k: 0.5 * cx[pl.ds(k * ny, ny), :],
            ratio,
            *(put(ref, f) for ref in (xi, xm, xu, xq, xr)),
        )
        for v in range(4):
            xown[v, f] = own[v]
        own = factor(
            ny,
            lambda k: lat[pl.ds(k, nx, stride=ny), :],
            lambda k: 0.5 * cy[pl.ds(k, nx, stride=ny), :],
            ratio,
            *(put(ref, f) for ref in (yi, ym, yu, yq, yr)),
        )
        for v in range(4):
            yown[v, f] = own[v]


def slope_kernel(axis, own, near, out):
    for f in range(2):
        out[f] = pair_source(axis, None, coefs_of(own, f), coefs_of(near, f))[1]


class Ghost:
    def __init__(self, shape, nx):
        self.shape, self.nx = shape, nx
        self.first = lax.broadcasted_iota(jnp.int32, shape, 1) < shape[1] // 2
        self.ratio = jnp.where(self.first, RATIOS[0], RATIOS[1])

    def lane(self, tiles, plane, k):
        at = self.nx * plane + k
        column = tiles[at // self.shape[1], :, at % self.shape[1] : at % self.shape[1] + 1]
        return jnp.broadcast_to(column, self.shape)

    def fields(self, tiles, plane, k):
        return jnp.where(self.first, self.lane(tiles, plane, k), self.lane(tiles, plane + 1, k))

    def named(self, tiles, name, k):
        return self.lane(tiles, 4 + PLANES.index(name), k)


def lateral_step(v, lateral, half):
    ny = v.shape[0]
    me, n = lax.axis_index("gy"), lax.axis_size("gy")
    row = lax.broadcasted_iota(jnp.int32, v.shape, 0)
    ahead = jnp.where(row == ny - 1, 0.0, pltpu.roll(v, ny - 1, 0))
    behind = jnp.where(row == 0, 0.0, pltpu.roll(v, 1, 0))
    east, west = lateral - half, lateral + half
    inside_high = (row == ny - 1) & (me < n - 1)
    inside_low = (row == 0) & (me > 0)
    side = jnp.where(inside_high, east, jnp.where(inside_low, west, 0.0))
    return east * (ahead - v) + west * (behind - v), side


def vertical_step(nz, v, column, lateral, half):
    upper = lax.axis_index("gz")
    lane = lax.broadcasted_iota(jnp.int32, v.shape, 1)
    column = jnp.broadcast_to(column, v.shape)
    ahead = jnp.where(lane == nz - 1, jnp.where(upper == 0, column, 0.0), pltpu.roll(v, nz - 1, 1))
    behind = jnp.where(lane == 0, jnp.where(upper == 0, 0.0, column), pltpu.roll(v, 1, 1))
    return (lateral - half) * (ahead - v) + (lateral + half) * (behind - v)


def ghost_kernel(nx, tiles, gi, gm, gu, gq, gr, own):
    ghost = Ghost(tiles.shape[1:], nx)

    def keep(ref):
        def store(k, v):
            ref[k] = v

        return store

    ports = factor(
        nx,
        lambda k: ghost.named(tiles, "lat", k),
        lambda k: 0.5 * ghost.named(tiles, "cx", k),
        ghost.ratio,
        *(keep(ref) for ref in (gi, gm, gu, gq, gr)),
    )
    for v in range(4):
        own[v] = ports[v]


def early_kernel(
    nx, nz, t, h, load, lat, up, cy, cz, mine, tiles, d, side, gd, gside
):
    upper = lax.axis_index("gz")
    ghost = Ghost(tiles.shape[1:], nx)
    for k in range(nx):
        v = ghost.fields(tiles, 0, k)
        lateral = ghost.ratio * ghost.named(tiles, "lat", k)
        step, gside[k] = lateral_step(v, lateral, 0.5 * ghost.named(tiles, "cy", k))
        inner, here = ghost.fields(tiles, 2, k), ghost.fields(mine, 0, k)
        ahead, behind = jnp.where(upper == 0, inner, here), jnp.where(upper == 0, here, inner)
        rise, half = ghost.ratio * ghost.named(tiles, "up", k), 0.5 * ghost.named(tiles, "cz", k)
        step = step + ((rise - half) * (ahead - v) + (rise + half) * (behind - v))
        gd[k] = v + step + jnp.where(ghost.first, ghost.named(tiles, "load", k), 0.0)
    for f, (ratio, ref) in enumerate(zip(RATIOS, (t, h))):
        for k in range(nx):
            v = ref[k]
            step, side[f, k] = lateral_step(v, ratio * lat[k], 0.5 * cy[k])
            at = nx * f + k
            out = v + step + vertical_step(
                nz, v, tiles[0, :, at : at + 1], ratio * up[k], 0.5 * cz[k]
            )
            d[f, k] = out + load[k] if f == 0 else out


def first_kernel(
    paired, nx, ny, faces, d0, side, gd, gside, xi, xm, xu, gi, gm, gu, own, near, gown, gnear,
    d, p, gp, ends, *word
):
    odd = lax.axis_index("gy") % 2
    half = ny // 2
    slopes = []
    for f in range(2):
        for k in range(nx):
            low = faces[1 - odd, f, pl.ds(k, half, stride=0), :]
            high = faces[odd, f, pl.ds(k, half, stride=0), :]
            d[f, k, :half] = d0[f, k, :half] + side[f, k, :half] * low
            d[f, k, half:] = d0[f, k, half:] + side[f, k, half:] * high
        mine = sweep(
            nx, lambda k: d[f, k], lambda k: xi[f, k], lambda k: xm[f, k], lambda k: xu[f, k], put(p, f)
        )
        ends[2 * f], ends[2 * f + 1] = mine
        if paired:
            word[0][f], slope = pair_source("gx", mine, coefs_of(own, f), coefs_of(near, f))
            slopes.append(slope)
    low_row = faces[1 - odd, 2, pl.ds(ny - 1, half, stride=0), :]
    high_row = faces[odd, 2, pl.ds(0, half, stride=0), :]
    first = lax.broadcasted_iota(jnp.int32, low_row.shape, 1) < low_row.shape[1] // 2

    def spread(row, k):
        a = jnp.broadcast_to(row[:, k : k + 1], row.shape)
        b = jnp.broadcast_to(row[:, nx + k : nx + k + 1], row.shape)
        return jnp.where(first, a, b)

    def rhs(k):
        beside_rows = jnp.concatenate([spread(low_row, k), spread(high_row, k)])
        return gd[k] + gside[k] * beside_rows

    def keep(k, v):
        gp[k] = v

    mine = sweep(nx, rhs, lambda k: gi[k], lambda k: gm[k], lambda k: gu[k], keep)
    ends[4] = packed(*mine)
    if paired:
        word[0][2] = packed(*pair_source("gx", mine, x_coefs(own, gown, 2), x_coefs(near, gnear, 2)))
        word[0][3] = jnp.where(place("gx")[2] == 0, slopes[0], slopes[1])


def packed(a, b):
    lane = lax.broadcasted_iota(jnp.int32, a.shape, 1)
    return jnp.where((lane & 32) == 0, a, b)


def unpacked(both):
    lane = lax.broadcasted_iota(jnp.int32, both.shape, 1)
    a = jnp.where((lane & 32) == 0, both, pltpu.roll(both, 32, 1))
    b = jnp.where((lane & 32) == 0, pltpu.roll(both, both.shape[1] - 32, 1), both)
    return a, b


def x_ends(ends, f):
    return (ends[2 * f], ends[2 * f + 1]) if f < 2 else unpacked(ends[4])


def x_coefs(own, ghost, f):
    return coefs_of(own, f) if f < 2 else tuple(ghost[v] for v in range(4))


def second_kernel(
    paired, nx, ny, nz, p, q, r, gp, gq, gr, ends, near_ends, own, near, gown, gnear,
    d, load, up, cz, yi, ym, yu, yown, ynear, *rest,
):
    far, (py, *outs, s) = rest[: 1 + paired[0]], rest[1 + paired[0] :]

    def values(f):
        mine, coefs = x_ends(ends, f), x_coefs(own, gown, f)
        if paired[0]:
            two, three = far
            if f < 2:
                word = two[f] + three[f], jnp.where(place("gx")[2] == f, two[3], three[3])
            else:
                word, more = unpacked(two[2]), unpacked(three[2])
                word = word[0] + more[0], word[1]
            other, other_coefs = x_ends(near_ends, f), x_coefs(near, gnear, f)
            return pair_values("gx", mine, other, coefs, other_coefs, word)

        def port_of(j):
            theirs = x_ends(far[0].at[j], f)
            at = [5 + 2 * v + f if f < 2 else 13 + v for v in range(4)]
            return tuple(theirs) + tuple(far[0][j, i] for i in at)

        return scan_values("gx", tuple(mine) + coefs, port_of)

    ghost_low, ghost_high = values(2)
    beyond = [gp[k] + gq[k] * ghost_low + gr[k] * ghost_high for k in range(nx)]
    for f, ratio in enumerate(RATIOS):
        low, high = values(f)
        for k in range(nx):
            v = p[f, k] + q[f, k] * low + r[f, k] * high
            at = f * nz // 2
            out = 2.0 * v - d[f, k]
            out = out + vertical_step(nz, v, beyond[k][:, at : at + 1], ratio * up[k], 0.5 * cz[k])
            if f == 0:
                out = out + load[k]
            s[f, pl.ds(k * ny, ny), :] = out
        mine = sweep(
            ny,
            lambda k: s[f, pl.ds(k, nx, stride=ny), :],
            lambda k: yi[f, k],
            lambda k: ym[f, k],
            lambda k: yu[f, k],
            put(py, f),
        )
        outs[0][2 * f], outs[0][2 * f + 1] = mine
        if paired[1]:
            outs[1][f] = pair_source("gy", mine, coefs_of(yown, f), coefs_of(ynear, f))[0]


def word_kernel(ends, own, slopes, out):
    for f in range(2):
        out[f] = near_word("gy", (ends[2 * f], ends[2 * f + 1]), coefs_of(own, f), slopes[f])


def new_kernel(paired, nx, ny, p, q, r, ends, word, own, near, slopes, *rest):
    received, news = rest[:-2], rest[-2:]
    for f, ref in enumerate(news):
        mine = (ends[2 * f], ends[2 * f + 1])
        coefs = coefs_of(own, f)
        if paired:
            two, three = received
            far = two[f] + three[f], slopes[f]
            low, high = word_values("gy", mine, word[f], coefs, coefs_of(near, f), far)
        else:
            (ports,) = received

            def port_of(j):
                return (ports[j, 2 * f], ports[j, 2 * f + 1]) + tuple(
                    ports[j, 4 + 2 * v + f] for v in range(4)
                )

            low, high = scan_values("gy", mine + coefs, port_of)
        for k in range(ny):
            ref[pl.ds(k, nx, stride=ny), :] = p[f, k] + q[f, k] * low + r[f, k] * high


def neighbours(one, two):
    across, n = lax.axis_size("gx"), lax.axis_size("gy")

    def swapped(first, value):
        partner = {i: i ^ 1 if first == 0 else ((i + 1) ^ 1) - 1 for i in range(n)}
        pairs = []
        for x in range(across):
            for i in range(n):
                j = partner[i]
                target = (x, j) if 0 <= j < n else (x ^ 1, i)
                if target[0] < across:
                    pairs.append((x * n + i, target[0] * n + target[1]))
        return lax.ppermute(value, ("gx", "gy"), pairs)

    return swapped(0, one), swapped(1, two)


def body(thermal, vapour, load, lat, up, cx, cy, cz):
    nx, ny, nz = thermal.shape
    assert lax.axis_size("gz") == 2 and nx * 8 == nz
    flat = (nx * ny, nz)
    lines_x, lines_y = (2, nx, ny, nz), (2, ny, nx, nz)
    block_x, block_y = (ny, nz), (nx, nz)
    paired = (lax.axis_size("gx") == 4, lax.axis_size("gy") == 4)
    thermal, vapour, load, lat, up, cx, cy, cz, mine = call(
        functools.partial(open_kernel, nx, nz),
        (thermal.shape,) * 8 + ((2,) + block_x,),
        *(
            pltpu.with_memory_space_constraint(a, pltpu.HBM)
            for a in (thermal, vapour, load, lat, up, cx, cy, cz)
        ),
        scratch=[pltpu.SemaphoreType.DMA((8,))],
        space=pltpu.HBM,
    )
    tiles = swap(mine, "gz", 1)
    xi, xm, xu, xq, xr, yi, ym, yu, yq, yr, xown, yown, one, two = call(
        functools.partial(coef_kernel, nx, ny),
        (lines_x,) * 5
        + (lines_y,) * 5
        + ((4, 2) + block_x, (4, 2) + block_y, (2,) + block_y, (2,) + block_y),
        *(a.reshape(flat) for a in (thermal, vapour, lat, cx, cy)),
    )
    xnear, ynear, yslopes = xown, yown, yown[0]
    if paired[0]:
        xnear = swap(xown, "gx", 1)
    if paired[1]:
        ynear = swap(yown, "gy", 1)
        (yslopes,) = call(functools.partial(slope_kernel, "gy"), ((2,) + block_y,), yown, ynear)
        yslopes = swap(yslopes, "gy", 2)
    one, two = neighbours(
        jnp.concatenate([one, tiles[:1]]), jnp.concatenate([two, tiles[:1]])
    )
    gi, gm, gu, gq, gr, gown = call(
        functools.partial(ghost_kernel, nx), ((nx,) + block_x,) * 5 + ((4,) + block_x,), tiles
    )
    d, side, gd, gside = call(
        functools.partial(early_kernel, nx, nz),
        (lines_x, lines_x) + ((nx,) + block_x,) * 2,
        thermal, vapour, load, lat, up, cy, cz, mine, tiles,
    )
    gnear = swap(gown, "gx", 1) if paired[0] else gown
    d, p, gp, ends, *word = call(
        functools.partial(first_kernel, paired[0], nx, ny),
        (lines_x, lines_x, (nx,) + block_x, (5,) + block_x) + ((4,) + block_x,) * paired[0],
        jnp.stack([one, two]), d, side, gd, gside, xi, xm, xu, gi, gm, gu, xown, xnear, gown, gnear,
    )
    if paired[0]:
        near_ends = swap(ends, "gx", 1)
        far = [swap(word[0], "gx", k) for k in (2, 3)]
    else:
        near_ends, far = ends, [everyones("gx", ends, xown, gown)]
    py, yends, *outs = call(
        functools.partial(second_kernel, paired, nx, ny, nz),
        (lines_y, (4,) + block_y) + (((2,) + block_y,) if paired[1] else ()),
        p, xq, xr, gp, gq, gr, ends, near_ends, xown, xnear, gown, gnear,
        d, load, up, cz, yi, ym, yu, yown, ynear, *far,
        scratch=[pltpu.VMEM((2,) + flat, F32)],
    )
    if paired[1]:
        received = [swap(outs[0], "gy", k) for k in (2, 3)]
        (word,) = call(word_kernel, ((2,) + block_y,), yends, yown, yslopes)
        word = swap(word, "gy", 1)
    else:
        word, received = yends, [everyones("gy", yends, yown)]
    t_new, h_new = call(
        functools.partial(new_kernel, paired[1], nx, ny),
        (flat, flat),
        py, yq, yr, yends, word, yown, ynear, yslopes, *received,
    )
    return t_new.reshape(thermal.shape), h_new.reshape(thermal.shape)


def solution(mesh):
    spec = P("gx", "gy", "gz")
    return jax.shard_map(
        body, mesh=mesh, in_specs=(spec,) * 8, out_specs=(spec, spec), check_vma=False
    )
```
